128 devices in a mesh: sx: 8 (over y, z_lo), sz: 16 (over x, z_hi, core).
Axes of the slice: x: 4, y: 4, z: 4 (z_hi: 2, z_lo: 2; z = z_hi * 2 + z_lo), core: 2. Of those that a mesh axis runs over, the one named last changes fastest.
Arguments:
- right_side: float32 [72, 256, 4096], P('sx', 'sz'), may hold values from -6 to 6
- coupling: bfloat16 [72, 5, 256, 256], P('sx'), may hold values from -0.15625 to 0.15625
- harmonic_offsets: int32 [5], replicated, may hold values from -6 to 6, as said below
- eigen_basis: bfloat16 [256, 256], replicated, may hold values from -0.375 to 0.375
- eigen_inverse: bfloat16 [256, 256], replicated, may hold values from -0.375 to 0.375
- eigen_size: float32 [256], replicated, may hold values from 0.5 to 50
Outputs:
- solution: float32 [72, 256, 4096], P('sx', 'sz')
The draws below stay inside these ranges and needn't reach their ends.
Inputs may be any that keep to these rules, and one draw needn't show every extreme that they name: `harmonic_offsets`: the offsets are distinct; some offset equals 6 and some equals -6.
All inputs are finite; a program needn't handle non-finite values.
Results may differ from the reference program's by a relative error of at most 0.00065.
The reference program's roundings to bfloat16 on the way (of `rounded`, `scaled` and `search`) count: a program that leaves them out, or rounds other values in their place, can miss the bound.
Values may be sent and summed in bfloat16 or wider, within the bound.
A program may use at most 128 MiB of HBM per device.

```python
import math
import jax
import jax.numpy as jnp
from jax import lax

KX = 72
KZ = 128
NC = 256
H = 5
OFF = 6
STEPS = 2
R = 32


def draw_harmonic_offsets(key, part):
    pick_key = jax.random.fold_in(key, 11)
    order_key = jax.random.fold_in(key, 23)
    middle = jnp.arange(-OFF + 1, OFF, dtype=jnp.int32)
    picked = jax.random.permutation(pick_key, middle)[:H - 2].astype(jnp.int32)
    ends = jnp.array([OFF, -OFF], dtype=jnp.int32)
    whole = jnp.concatenate([ends, picked])
    order = jax.random.permutation(order_key, H)
    return whole[order].astype(jnp.int32)


def shard_levels(key, extent, split, smallest, largest):
    def one(position, blocks):
        heights = jax.random.uniform(jax.random.fold_in(jax.random.fold_in(key, 6), position), (blocks,), jnp.float32, smallest / len(split), largest / len(split))
        return jnp.repeat(jnp.exp(heights), extent[position] // blocks).reshape((-1,) + (1,) * (len(extent) - position - 1))

    gain = one(*split[0])
    for cut in split[1:]:
        gain = gain * one(*cut)
    return gain


def scatter_about(key, extent, deviation, bound, split=(), held_as=jnp.bfloat16):
    entries = jax.random.normal(key, extent, jnp.float32) * deviation
    if len(split) > 0:
        entries = shard_levels(key, extent, split, -0.22, 0.18) * entries
    return jnp.clip(entries, min=-bound, max=bound).astype(held_as)


def setup_inputs(seed: int = 0) -> dict:
    key_list = jax.random.split(jax.random.key(seed), 7)
    right_side = scatter_about(key_list[0], (KX, NC, KZ * R), 1.0, 6.0, ((0, 8), (1, 16)), jnp.float32)
    coupling = scatter_about(key_list[1], (KX, H, NC, NC), (H * NC) ** -0.5, 0.15625, ((0, 8),))
    harmonic_offsets = draw_harmonic_offsets(jax.random.fold_in(key_list[6], 71), 0)
    eigen_basis = scatter_about(key_list[3], (NC, NC), NC ** -0.5, 0.375)
    eigen_inverse = scatter_about(key_list[4], (NC, NC), NC ** -0.5, 0.375)
    eigen_size = jnp.clip(jnp.exp(jax.random.uniform(key_list[5], (NC,), jnp.float32, math.log(0.5), math.log(50.0))), 0.5, 50.0)
    return {"right_side": right_side, "coupling": coupling, "harmonic_offsets": harmonic_offsets, "eigen_basis": eigen_basis, "eigen_inverse": eigen_inverse, "eigen_size": eigen_size}


def wave_grid():
    modes = jnp.arange(KX, dtype=jnp.int32)
    spans = jnp.arange(KZ, dtype=jnp.int32)
    signed_x = jnp.where(modes < KX // 2, modes, modes - KX).astype(jnp.float32) * (4.0 / KX)
    signed_z = jnp.where(spans < KZ // 2, spans, spans - KZ).astype(jnp.float32) * (4.0 / KZ)
    table = 1.0 + signed_x[:, None] ** 2 + signed_z[None, :] ** 2
    return jnp.repeat(table, R, axis=1)


def reference(right_side, coupling, harmonic_offsets, eigen_basis, eigen_inverse, eigen_size):
    wave_square = wave_grid()

    def precond_mode(pair):
        res_mode, wave_mode = pair
        rounded = res_mode.astype(jnp.bfloat16)
        spectral = jnp.dot(eigen_inverse, rounded, preferred_element_type=jnp.float32)
        factor = -1.0 / (eigen_size[:, None] + wave_mode[None, :])
        scaled = (spectral * factor).astype(jnp.bfloat16)
        result = jnp.dot(eigen_basis, scaled, preferred_element_type=jnp.float32)
        return result.astype(jnp.bfloat16)

    residual = right_side
    solution = jnp.zeros_like(right_side)
    for sweep in range(STEPS):
        search = lax.map(precond_mode, (residual, wave_square))

        def apply_mode(mode):
            wave_mode = lax.dynamic_index_in_dim(wave_square, mode, 0, keepdims=False)
            own = lax.dynamic_index_in_dim(search, mode, 0, keepdims=False)
            accum = -wave_mode[None, :] * own.astype(jnp.float32)
            blocks = lax.dynamic_index_in_dim(coupling, mode, 0, keepdims=False)
            for harmonic in range(H):
                target = ((mode + harmonic_offsets[harmonic]) % KX).astype(jnp.int32)
                source = lax.dynamic_index_in_dim(search, target, 0, keepdims=False)
                accum = accum + jnp.dot(blocks[harmonic], source, preferred_element_type=jnp.float32)
            return accum

        image = lax.map(apply_mode, jnp.arange(KX, dtype=jnp.int32))
        aligned = jnp.sum(jnp.sum(image * residual, axis=(0, 1)).reshape(KZ, R), axis=0)
        energy = jnp.sum(jnp.sum(image * image, axis=(0, 1)).reshape(KZ, R), axis=0)
        step_size = jnp.tile(aligned / (energy + 1e-6), KZ)
        solution = solution + step_size * search.astype(jnp.float32)
        residual = residual - step_size * image
    return solution
```

```python
import jax
import jax.numpy as jnp
from jax import lax
from jax.experimental import pallas as pl
from jax.experimental.pallas import tpu as pltpu
from jax.sharding import PartitionSpec as P

KX = 72
KZ = 128
NC = 256
H = 5
OFF = 6
R = 32
NX = 8
NZ = 16
M = KX // NX
ROWS = NC // NZ
COLS = KZ * R // NZ
SPANS = KZ // NZ
MESH = pl.DeviceIdType.MESH
PARTS_OF = ((0,), (1, 2), (3,))

CHUNK = 3
CHUNKS = M // CHUNK


def flip(place):
    return 2 - 4 * ((place // 2) % 2)


def group_of(sx, sz):
    return sz + ((sx // 2) % 2) * flip(sz)


def wave_row(sx, mode, group):
    index = sx * M + mode
    signed_x = jnp.where(index < KX // 2, index, index - KX).astype(jnp.float32) * (4.0 / KX)
    column = lax.broadcasted_iota(jnp.int32, (1, COLS), 1)
    span = group * SPANS + column // R
    signed_z = jnp.where(span < KZ // 2, span, span - KZ).astype(jnp.float32) * (4.0 / KZ)
    return 1.0 + signed_x * signed_x + signed_z * signed_z


def kernel(
    offsets, right, coupling, basis, inverse, sizes, out,
    start, factor, image, residual, blocks,
    search, back, final, sums, parts, row_sums, row_total, all_sums,
    load_sem, in_send, in_recv, move_send, move_recv, halo_send, halo_recv, row_send, row_recv, all_send, all_recv, local_sem, out_sem,
):
    sx, sz = lax.axis_index("sx"), lax.axis_index("sz")
    low_z = sx % 2
    group = group_of(sx, sz)
    up = ((sx + 1) % NX, sz + low_z * flip(sz))
    down = ((sx + NX - 1) % NX, sz + (1 - low_z) * flip(sz))
    twisted = (low_z * up[0] + (1 - low_z) * down[0], sz + flip(sz))

    load_blocks = pltpu.make_async_copy(coupling, blocks, load_sem.at[0])
    load_blocks.start()

    barrier = pltpu.get_barrier_semaphore()

    @pl.loop(1, NZ)
    def _(k):
        pl.semaphore_signal(barrier, inc=1, device_id=(sx, (sz + k) % NZ), device_id_type=MESH)

    @pl.loop(1, NX)
    def _(k):
        pl.semaphore_signal(barrier, inc=1, device_id=((sx + k) % NX, sz), device_id_type=MESH)

    pl.semaphore_signal(barrier, inc=1, device_id=twisted, device_id_type=MESH)

    pl.semaphore_wait(barrier, NZ - 1 + NX - 1 + 1)

    def columns(place):
        return pl.ds(pl.multiple_of(place * COLS, COLS), COLS)

    def rows(place):
        return pl.ds(pl.multiple_of(place * ROWS, ROWS), ROWS)

    def modes(chunk):
        return pl.ds(chunk * CHUNK, CHUNK)

    def inward(chunk, k):
        to = (sz + k) % NZ
        return pltpu.make_async_remote_copy(
            src_ref=right.at[modes(chunk), :, columns(group_of(sx, to))],
            dst_ref=start.at[modes(chunk), rows(sz), :],
            send_sem=in_send.at[chunk, k],
            recv_sem=in_recv.at[chunk, k],
            device_id=(sx, to),
            device_id_type=MESH,
        )

    def outward(step, k):
        to = (sz + k) % NZ
        return pltpu.make_async_remote_copy(
            src_ref=search.at[step, pl.ds(OFF, M), rows(to), :],
            dst_ref=back.at[step, :, :, columns(group)],
            send_sem=move_send.at[step, k],
            recv_sem=move_recv.at[step, k],
            device_id=(sx, to),
            device_id_type=MESH,
        )

    def halo(step, part):
        to, begin, end = (
            (down, 0, M), (down, 3, M + 3), (up, 3, -OFF + 0), (up, 6, -OFF + 3),
        )[part]
        return pltpu.make_async_remote_copy(
            src_ref=search.at[step, pl.ds(OFF + begin, 3)],
            dst_ref=search.at[step, pl.ds(OFF + end, 3)],
            send_sem=halo_send.at[step, part],
            recv_sem=halo_recv.at[step, part],
            device_id=to,
            device_id_type=MESH,
        )

    for chunk in range(CHUNKS):

        @pl.loop(1, NZ)
        def _(k):
            inward(chunk, k).start()

    own = pltpu.make_async_copy(right.at[:, :, columns(group)], start.at[:, rows(sz), :], local_sem.at[0])
    own.start()

    @pl.loop(0, M)
    def _(m):
        factor[m] = -1.0 / (sizes[...] + wave_row(sx, m, group))

    own.wait()

    def precondition(step, m, rounded):
        spectral = jnp.dot(inverse[...], rounded, preferred_element_type=jnp.float32)
        scaled = (spectral * factor[m]).astype(jnp.bfloat16)
        result = jnp.dot(basis[...], scaled, preferred_element_type=jnp.float32)
        search[step, OFF + m] = result.astype(jnp.bfloat16)

    def apply(step):
        for part in range(4):
            halo(step, part).wait_recv()
        sums[...] = jnp.zeros_like(sums)

        @pl.loop(0, M)
        def _(m):
            total = -wave_row(sx, m, group) * search[step, OFF + m].astype(jnp.float32)
            for h in range(H):
                total = total + jnp.dot(
                    blocks[m, h], search[step, OFF + m + offsets[h]], preferred_element_type=jnp.float32
                )
            if step == 0:
                image[m] = total
                before = start[m]
            else:
                before = residual[m]
            sums[0] += jnp.sum((total * before).reshape(NC // 8, 8, COLS), axis=0)
            sums[1] += jnp.sum((total * total).reshape(NC // 8, 8, COLS), axis=0)

    def row_copy(step, k):
        to = (sz + k) % NZ
        return pltpu.make_async_remote_copy(
            src_ref=parts.at[step],
            dst_ref=row_sums.at[step, sz],
            send_sem=row_send.at[step, k],
            recv_sem=row_recv.at[step, k],
            device_id=(sx, to),
            device_id_type=MESH,
        )

    def all_copy(step, k):
        to = (sx + k) % NX
        return pltpu.make_async_remote_copy(
            src_ref=row_total.at[step],
            dst_ref=all_sums.at[step, sx],
            send_sem=all_send.at[step, k],
            recv_sem=all_recv.at[step, k],
            device_id=(to, sz),
            device_id_type=MESH,
        )

    first_half = lax.broadcasted_iota(jnp.int32, (8, 128), 1) < 64

    def step_size(step):
        def fold(value):
            value = value[:, :128] + value[:, 128:]
            value = value + pltpu.roll(value, 64, 1)
            return value + pltpu.roll(value, 32, 1)

        both = jnp.where(first_half, fold(sums[0]), fold(sums[1]))
        mine = jnp.sum(both, axis=0, keepdims=True)
        parts[step] = mine
        row_sums[step, sz] = mine

        @pl.loop(1, NZ)
        def _(k):
            row_copy(step, k).start()

        @pl.loop(1, NZ)
        def _(k):
            row_copy(step, k).wait_recv()

        of_row = row_sums[step, 0]
        for place in range(1, NZ):
            of_row = of_row + row_sums[step, place]
        row_total[step] = of_row
        all_sums[step, sx] = of_row

        @pl.loop(1, NX)
        def _(k):
            all_copy(step, k).start()

        @pl.loop(1, NX)
        def _(k):
            all_copy(step, k).wait_recv()

        of_all = all_sums[step, 0]
        for place in range(1, NX):
            of_all = of_all + all_sums[step, place]
        of_all = jnp.broadcast_to(of_all, (8, 128))
        other = pltpu.roll(of_all, 64, 1)
        aligned = jnp.where(first_half, of_all, other)
        energy = jnp.where(first_half, other, of_all)
        return (aligned / (energy + 1e-6))[0:1]

    for chunk in range(CHUNKS):

        @pl.loop(1, NZ)
        def _(k):
            inward(chunk, k).wait_recv()

        @pl.loop(chunk * CHUNK, chunk * CHUNK + CHUNK)
        def _(m):
            precondition(0, m, start[m].astype(jnp.bfloat16))

        for part in PARTS_OF[chunk]:
            halo(0, part).start()

    @pl.loop(1, NZ)
    def _(k):
        outward(0, k).start()

    own_first = pltpu.make_async_copy(
        search.at[0, pl.ds(OFF, M), rows(sz), :], back.at[0, :, :, columns(group)], local_sem.at[1]
    )
    own_first.start()

    load_blocks.wait()

    apply(0)
    first = step_size(0)
    first_wide = jnp.concatenate([first, first], axis=1)

    for chunk in range(CHUNKS):

        @pl.loop(chunk * CHUNK, chunk * CHUNK + CHUNK)
        def _(m):
            left = start[m] - first_wide * image[m]
            residual[m] = left
            precondition(1, m, left.astype(jnp.bfloat16))

        for part in PARTS_OF[chunk]:
            halo(1, part).start()

    @pl.loop(1, NZ)
    def _(k):
        outward(1, k).start()

    own_second = pltpu.make_async_copy(
        search.at[1, pl.ds(OFF, M), rows(sz), :], back.at[1, :, :, columns(group)], local_sem.at[2]
    )
    own_second.start()
    apply(1)
    second = step_size(1)

    own_first.wait()
    own_second.wait()

    @pl.loop(1, NZ)
    def _(k):
        outward(0, k).wait_recv()
        outward(1, k).wait_recv()

    reach = KZ * R // 128
    first_all = jnp.tile(first, (1, reach))
    second_all = jnp.tile(second, (1, reach))

    @pl.loop(0, M)
    def _(m):
        final[m] = first_all * back[0, m].astype(jnp.float32) + second_all * back[1, m].astype(jnp.float32)
        pltpu.make_async_copy(final.at[m], out.at[m], out_sem.at[m]).start()

    @pl.loop(1, NZ)
    def _(k):
        for chunk in range(CHUNKS):
            inward(chunk, k).wait_send()
        outward(0, k).wait_send()
        outward(1, k).wait_send()
        row_copy(0, k).wait_send()
        row_copy(1, k).wait_send()

    @pl.loop(1, NX)
    def _(k):
        all_copy(0, k).wait_send()
        all_copy(1, k).wait_send()

    for step in range(2):
        for part in range(4):
            halo(step, part).wait_send()

    @pl.loop(0, M)
    def _(m):
        pltpu.make_async_copy(final.at[m], out.at[m], out_sem.at[m]).wait()


def shards(right_side, coupling, harmonic_offsets, eigen_basis, eigen_inverse, eigen_size):
    vmem = pl.BlockSpec(memory_space=pltpu.VMEM)
    anywhere = pl.BlockSpec(memory_space=pl.ANY)
    low, full = jnp.bfloat16, jnp.float32
    dma = pltpu.SemaphoreType.DMA
    return pl.pallas_call(
        kernel,
        out_shape=jax.ShapeDtypeStruct((M, ROWS, KZ * R), full),
        in_specs=[pl.BlockSpec(memory_space=pltpu.SMEM), anywhere, anywhere, vmem, vmem, vmem],
        out_specs=anywhere,
        scratch_shapes=[
            pltpu.VMEM((M, NC, COLS), full),
            pltpu.VMEM((M, NC, COLS), full),
            pltpu.VMEM((M, NC, COLS), full),
            pltpu.VMEM((M, NC, COLS), full),
            pltpu.VMEM((M, H, NC, NC), low),
            pltpu.VMEM((2, M + 2 * OFF, NC, COLS), low),
            pltpu.VMEM((2, M, ROWS, KZ * R), low),
            pltpu.VMEM((M, ROWS, KZ * R), full),
            pltpu.VMEM((2, 8, COLS), full),
            pltpu.VMEM((2, 1, 128), full),
            pltpu.VMEM((2, NZ, 1, 128), full),
            pltpu.VMEM((2, 1, 128), full),
            pltpu.VMEM((2, NX, 1, 128), full),
            dma((1,)),
            dma((CHUNKS, NZ)),
            dma((CHUNKS, NZ)),
            dma((2, NZ)),
            dma((2, NZ)),
            dma((2, 4)),
            dma((2, 4)),
            dma((2, NZ)),
            dma((2, NZ)),
            dma((2, NX)),
            dma((2, NX)),
            dma((3,)),
            dma((M,)),
        ],
        compiler_params=pltpu.CompilerParams(
            collective_id=0, has_side_effects=True, vmem_limit_bytes=56 * 2**20
        ),
    )(harmonic_offsets, right_side, coupling, eigen_basis, eigen_inverse, eigen_size.reshape(NC, 1))


def solution(mesh):
    in_specs = (P("sx", "sz", None), P("sx", None, None, None), P(), P(), P(), P())
    out_specs = P("sx", "sz", None)
    return jax.shard_map(shards, mesh=mesh, in_specs=in_specs, out_specs=out_specs, check_vma=False)
```

```python
import jax
import jax.numpy as jnp
from jax import lax
from jax.experimental import pallas as pl
from jax.experimental.pallas import tpu as pltpu
from jax.sharding import PartitionSpec as P

KX = 72
KZ = 128
NC = 256
H = 5
OFF = 6
R = 32
NX = 8
NZ = 16
M = KX // NX
ROWS = NC // NZ
COLS = KZ * R // NZ
SPANS = KZ // NZ
MESH = pl.DeviceIdType.MESH
PACE = ((15, 0, 0, 0, 0), (15, 0, 0, 0, 0))
ORDER = (3, 4, 5, 0, 6, 1, 7, 2, 8)
WINDOW = 4


def flip(place):
    return 2 - 4 * ((place // 2) % 2)


def group_of(sx, sz):
    return sz + ((sx // 2) % 2) * flip(sz)


def wave_row(sx, mode, group):
    index = sx * M + mode
    signed_x = jnp.where(index < KX // 2, index, index - KX).astype(jnp.float32) * (4.0 / KX)
    column = lax.broadcasted_iota(jnp.int32, (1, COLS), 1)
    span = group * SPANS + column // R
    signed_z = jnp.where(span < KZ // 2, span, span - KZ).astype(jnp.float32) * (4.0 / KZ)
    return 1.0 + signed_x * signed_x + signed_z * signed_z


def kernel(
    offsets, right, coupling, basis, inverse, sizes, out,
    start, factor, image, residual, blocks,
    search, back, final, sums, parts, row_sums, row_total, all_sums,
    load_sem, in_send, in_recv, move_send, move_recv, halo_send, halo_recv, row_send, row_recv, all_send, all_recv, local_sem, out_sem,
):
    sx, sz = lax.axis_index("sx"), lax.axis_index("sz")
    low_z = sx % 2
    group = group_of(sx, sz)
    up = ((sx + 1) % NX, sz + low_z * flip(sz))
    down = ((sx + NX - 1) % NX, sz + (1 - low_z) * flip(sz))
    twisted = (low_z * up[0] + (1 - low_z) * down[0], sz + flip(sz))

    load_blocks = pltpu.make_async_copy(coupling, blocks, load_sem.at[0])
    load_blocks.start()

    barrier = pltpu.get_barrier_semaphore()

    @pl.loop(1, NZ)
    def _(k):
        pl.semaphore_signal(barrier, inc=1, device_id=(sx, (sz + k) % NZ), device_id_type=MESH)

    @pl.loop(1, NX)
    def _(k):
        pl.semaphore_signal(barrier, inc=1, device_id=((sx + k) % NX, sz), device_id_type=MESH)

    pl.semaphore_signal(barrier, inc=1, device_id=twisted, device_id_type=MESH)

    pl.semaphore_wait(barrier, NZ - 1 + NX - 1 + 1)

    def columns(place):
        return pl.ds(pl.multiple_of(place * COLS, COLS), COLS)

    def rows(place):
        return pl.ds(pl.multiple_of(place * ROWS, ROWS), ROWS)

    def inward(m, k):
        to = (sz + k) % NZ
        return pltpu.make_async_remote_copy(
            src_ref=right.at[m, :, columns(group_of(sx, to))],
            dst_ref=start.at[m, rows(sz), :],
            send_sem=in_send.at[m],
            recv_sem=in_recv.at[m],
            device_id=(sx, to),
            device_id_type=MESH,
        )

    def send_mode(m):
        @pl.loop(1, NZ)
        def _(k):
            inward(m, k).start()

    def all_but_own(m, sem):
        part = start.at[m, pl.ds(0, NC - ROWS), :]
        return pltpu.make_async_copy(part, part, sem)

    def outward(step, k):
        to = (sz + k) % NZ
        return pltpu.make_async_remote_copy(
            src_ref=search.at[step, pl.ds(OFF, M), rows(to), :],
            dst_ref=back.at[step, :, :, columns(group)],
            send_sem=move_send.at[step, k],
            recv_sem=move_recv.at[step, k],
            device_id=(sx, to),
            device_id_type=MESH,
        )

    def send_share(step, stage):
        begin = 1 + sum(PACE[step][:stage])

        @pl.loop(begin, begin + PACE[step][stage])
        def _(k):
            outward(step, k).start()

    def send_one(step, stage, m):
        begin = 1 + sum(PACE[step][:stage])

        @pl.when(m < PACE[step][stage])
        def _():
            outward(step, begin + m).start()

    def halo(step, part):
        to, begin, end = (down, part, M + part) if part < OFF else (up, part - 3, part - 2 * OFF)
        return pltpu.make_async_remote_copy(
            src_ref=search.at[step, OFF + begin],
            dst_ref=search.at[step, OFF + end],
            send_sem=halo_send.at[step, part],
            recv_sem=halo_recv.at[step, part],
            device_id=to,
            device_id_type=MESH,
        )

    def send_halo(step, m):
        if m < OFF:
            halo(step, m).start()
        if m >= M - OFF:
            halo(step, m + 3).start()

    for m in ORDER[:WINDOW]:
        send_mode(m)

    own = pltpu.make_async_copy(right.at[:, :, columns(group)], start.at[:, rows(sz), :], local_sem.at[0])
    own.start()

    sizes_down = jnp.transpose(jnp.broadcast_to(sizes[...], (NC, NC)))

    @pl.loop(0, M)
    def _(m):
        factor[m] = -1.0 / (sizes_down + wave_row(sx, m, group))

    own.wait()

    def precondition(step, m, rounded):
        spectral = jnp.dot(inverse[...], rounded, preferred_element_type=jnp.float32)
        scaled = (spectral * factor[m]).astype(jnp.bfloat16)
        result = jnp.dot(basis[...], scaled, preferred_element_type=jnp.float32)
        search[step, OFF + m] = result.astype(jnp.bfloat16)

    def apply(step):
        for part in range(2 * OFF):
            halo(step, part).wait_recv()

        sums[...] = jnp.zeros_like(sums)

        @pl.loop(0, M)
        def _(m):
            send_one(step, 1, m)
            total = -wave_row(sx, m, group) * search[step, OFF + m].astype(jnp.float32)
            for h in range(H):
                total = total + jnp.dot(
                    blocks[m, h], search[step, OFF + m + offsets[h]], preferred_element_type=jnp.float32
                )
            if step == 0:
                image[m] = total
                before = start[m]
            else:
                before = residual[m]
            sums[0] += jnp.sum((total * before).reshape(NC // 8, 8, COLS), axis=0)
            sums[1] += jnp.sum((total * total).reshape(NC // 8, 8, COLS), axis=0)

    def row_copy(step, k):
        to = (sz + k) % NZ
        return pltpu.make_async_remote_copy(
            src_ref=parts.at[step],
            dst_ref=row_sums.at[step, sz],
            send_sem=row_send.at[step, k],
            recv_sem=row_recv.at[step, k],
            device_id=(sx, to),
            device_id_type=MESH,
        )

    def all_copy(step, k):
        to = (sx + k) % NX
        return pltpu.make_async_remote_copy(
            src_ref=row_total.at[step],
            dst_ref=all_sums.at[step, sx],
            send_sem=all_send.at[step, k],
            recv_sem=all_recv.at[step, k],
            device_id=(to, sz),
            device_id_type=MESH,
        )

    first_half = lax.broadcasted_iota(jnp.int32, (8, 128), 1) < 64

    def step_size(step):
        def fold(value):
            value = value[:, :128] + value[:, 128:]
            value = value + pltpu.roll(value, 64, 1)
            return value + pltpu.roll(value, 32, 1)

        both = jnp.where(first_half, fold(sums[0]), fold(sums[1]))
        mine = jnp.sum(both, axis=0, keepdims=True)
        parts[step] = mine
        row_sums[step, sz] = mine

        @pl.loop(1, NZ)
        def _(k):
            row_copy(step, k).start()

        send_share(step, 2)

        @pl.loop(1, NZ)
        def _(k):
            row_copy(step, k).wait_recv()

        of_row = row_sums[step, 0]
        for place in range(1, NZ):
            of_row = of_row + row_sums[step, place]
        row_total[step] = of_row
        all_sums[step, sx] = of_row

        @pl.loop(1, NX)
        def _(k):
            all_copy(step, k).start()

        send_share(step, 3)

        @pl.loop(1, NX)
        def _(k):
            all_copy(step, k).wait_recv()

        of_all = all_sums[step, 0]
        for place in range(1, NX):
            of_all = of_all + all_sums[step, place]
        of_all = jnp.broadcast_to(of_all, (8, 128))
        other = pltpu.roll(of_all, 64, 1)
        aligned = jnp.where(first_half, of_all, other)
        energy = jnp.where(first_half, other, of_all)
        return (aligned / (energy + 1e-6))[0:1]

    for place, m in enumerate(ORDER):
        all_but_own(m, in_recv.at[m]).wait()
        if place + WINDOW < M:
            send_mode(ORDER[place + WINDOW])
        precondition(0, m, start[m].astype(jnp.bfloat16))
        send_halo(0, m)

    send_share(0, 0)
    own_first = pltpu.make_async_copy(
        search.at[0, pl.ds(OFF, M), rows(sz), :], back.at[0, :, :, columns(group)], local_sem.at[1]
    )
    own_first.start()

    load_blocks.wait()

    apply(0)
    first = step_size(0)
    first_wide = jnp.concatenate([first, first], axis=1)

    for m in ORDER:
        left = start[m] - first_wide * image[m]
        residual[m] = left
        precondition(1, m, left.astype(jnp.bfloat16))
        send_halo(1, m)

    send_share(1, 0)
    own_second = pltpu.make_async_copy(
        search.at[1, pl.ds(OFF, M), rows(sz), :], back.at[1, :, :, columns(group)], local_sem.at[2]
    )
    own_second.start()
    apply(1)
    second = step_size(1)

    own_first.wait()
    own_second.wait()

    @pl.loop(1, NZ)
    def _(k):
        outward(0, k).wait_recv()
        outward(1, k).wait_recv()

    reach = KZ * R // 128
    first_all = jnp.tile(first, (1, reach))
    second_all = jnp.tile(second, (1, reach))

    @pl.loop(0, M)
    def _(m):
        final[m] = first_all * back[0, m].astype(jnp.float32) + second_all * back[1, m].astype(jnp.float32)
        pltpu.make_async_copy(final.at[m], out.at[m], out_sem.at[m]).start()

    @pl.loop(1, NZ)
    def _(k):
        outward(0, k).wait_send()
        outward(1, k).wait_send()
        row_copy(0, k).wait_send()
        row_copy(1, k).wait_send()

    @pl.loop(1, NX)
    def _(k):
        all_copy(0, k).wait_send()
        all_copy(1, k).wait_send()

    for m in range(M):
        all_but_own(m, in_send.at[m]).wait()

    for step in range(2):
        for part in range(2 * OFF):
            halo(step, part).wait_send()

    @pl.loop(0, M)
    def _(m):
        pltpu.make_async_copy(final.at[m], out.at[m], out_sem.at[m]).wait()


def shards(right_side, coupling, harmonic_offsets, eigen_basis, eigen_inverse, eigen_size):
    vmem = pl.BlockSpec(memory_space=pltpu.VMEM)
    anywhere = pl.BlockSpec(memory_space=pl.ANY)
    low, full = jnp.bfloat16, jnp.float32
    dma = pltpu.SemaphoreType.DMA
    return pl.pallas_call(
        kernel,
        out_shape=jax.ShapeDtypeStruct((M, ROWS, KZ * R), full),
        in_specs=[pl.BlockSpec(memory_space=pltpu.SMEM), anywhere, anywhere, vmem, vmem, vmem],
        out_specs=anywhere,
        scratch_shapes=[
            pltpu.VMEM((M, NC, COLS), full),
            pltpu.VMEM((M, NC, COLS), full),
            pltpu.VMEM((M, NC, COLS), full),
            pltpu.VMEM((M, NC, COLS), full),
            pltpu.VMEM((M, H, NC, NC), low),
            pltpu.VMEM((2, M + 2 * OFF, NC, COLS), low),
            pltpu.VMEM((2, M, ROWS, KZ * R), low),
            pltpu.VMEM((M, ROWS, KZ * R), full),
            pltpu.VMEM((2, 8, COLS), full),
            pltpu.VMEM((2, 1, 128), full),
            pltpu.VMEM((2, NZ, 1, 128), full),
            pltpu.VMEM((2, 1, 128), full),
            pltpu.VMEM((2, NX, 1, 128), full),
            dma((1,)),
            dma((M,)),
            dma((M,)),
            dma((2, NZ)),
            dma((2, NZ)),
            dma((2, 2 * OFF)),
            dma((2, 2 * OFF)),
            dma((2, NZ)),
            dma((2, NZ)),
            dma((2, NX)),
            dma((2, NX)),
            dma((3,)),
            dma((M,)),
        ],
        compiler_params=pltpu.CompilerParams(
            collective_id=0, has_side_effects=True, vmem_limit_bytes=56 * 2**20
        ),
    )(harmonic_offsets, right_side, coupling, eigen_basis, eigen_inverse, eigen_size.reshape(1, NC))


def solution(mesh):
    in_specs = (P("sx", "sz", None), P("sx", None, None, None), P(), P(), P(), P())
    out_specs = P("sx", "sz", None)
    return jax.shard_map(shards, mesh=mesh, in_specs=in_specs, out_specs=out_specs, check_vma=False)
```

```python
import jax
import jax.numpy as jnp
from jax import lax
from jax.experimental import pallas as pl
from jax.experimental.pallas import tpu as pltpu
from jax.sharding import PartitionSpec as P

KX = 72
KZ = 128
NC = 256
H = 5
OFF = 6
R = 32
NX = 8
NZ = 16
M = KX // NX
ROWS = NC // NZ
COLS = KZ * R // NZ
SPANS = KZ // NZ
QUARTER = NC // 4
MESH = pl.DeviceIdType.MESH
WINDOW = 4
PACE = ((15, 0, 0, 0, 0), (15, 0, 0, 0, 0))


def device_at(x, y, z, core):
    return 2 * y + z % 2, 4 * x + 2 * (z // 2) + core


def wave_row(block, mode, group):
    index = block * M + mode
    signed_x = jnp.where(index < KX // 2, index, index - KX).astype(jnp.float32) * (4.0 / KX)
    column = lax.broadcasted_iota(jnp.int32, (1, COLS), 1)
    span = group * SPANS + column // R
    signed_z = jnp.where(span < KZ // 2, span, span - KZ).astype(jnp.float32) * (4.0 / KZ)
    return 1.0 + signed_x * signed_x + signed_z * signed_z


def kernel(
    offsets, right, coupling, basis, inverse, sizes, out,
    start, factor, image, residual, blocks,
    search, back, final, sums, parts, row_sums, row_total, all_sums,
    load_sem, in_send, in_near, in_recv, out_send, out_near, out_recv, halo_send, halo_recv,
    block_send, block_recv, pass_send, row_send, row_recv, all_send, all_recv, final_sem,
):
    sx, sz = lax.axis_index("sx"), lax.axis_index("sz")
    y, low_z = sx // 2, sx % 2
    x, core = sz // 4, sz % 2
    z = 2 * ((sz // 2) % 2) + low_z
    block = 2 * y + core
    group = 4 * x + z
    at_home = core == low_z
    away = core != low_z
    other = sz + 1 - 2 * core
    up = ((sx + 2 * core) % NX, other)
    down = ((sx + NX - 2 * (1 - core)) % NX, other)
    across = ((sx + NX + 4 * core - 2) % NX, other)

    load_blocks = pltpu.make_async_copy(coupling, blocks, load_sem.at[0])

    @pl.when(at_home)
    def _():
        load_blocks.start()

    barrier = pltpu.get_barrier_semaphore()

    place = NZ * low_z + sz

    @pl.loop(1, 2 * NZ)
    def _(k):
        to = (place + k) % (2 * NZ)
        pl.semaphore_signal(barrier, inc=1, device_id=(2 * y + to // NZ, to % NZ), device_id_type=MESH)

    @pl.loop(1, NX)
    def _(k):
        pl.semaphore_signal(barrier, inc=1, device_id=((sx + k) % NX, sz), device_id_type=MESH)

    pl.semaphore_signal(barrier, inc=1, device_id=across, device_id_type=MESH)
    pl.semaphore_wait(barrier, 2 * NZ - 1 + NX - 1 + 1)

    def columns(index):
        return pl.ds(pl.multiple_of(index * COLS, COLS), COLS)

    def rows(index):
        return pl.ds(pl.multiple_of(index * ROWS, ROWS), ROWS)

    def quarter(index):
        return pl.ds(pl.multiple_of(index * QUARTER, QUARTER), QUARTER)

    def push(side):
        index = 2 * (x % 2) + side
        return pltpu.make_async_remote_copy(
            src_ref=coupling.at[:, :, quarter(index), :],
            dst_ref=blocks.at[:, :, quarter(index), :],
            send_sem=block_send.at[side],
            recv_sem=block_recv.at[index],
            device_id=device_at(x, y, (z + 1 + 2 * side) % 4, core),
            device_id_type=MESH,
        )

    def forward(side):
        index = 2 * (x % 2) + side
        return pltpu.make_async_remote_copy(
            src_ref=blocks.at[:, :, quarter(index), :],
            dst_ref=blocks.at[:, :, quarter(index), :],
            send_sem=pass_send.at[side],
            recv_sem=block_recv.at[index],
            device_id=(sx, (sz + 4 + 8 * side) % NZ),
            device_id_type=MESH,
        )

    def arrived(index):
        part = blocks.at[:, :, quarter(index), :]
        return pltpu.make_async_copy(part, part, block_recv.at[index])

    @pl.when(at_home)
    def _():
        for side in range(2):
            push(side).start()

    def inward(m, k, send_sem):
        to = (group + k) % NZ
        return pltpu.make_async_remote_copy(
            src_ref=right.at[m, :, columns(to)],
            dst_ref=start.at[m, rows(sz), :],
            send_sem=send_sem,
            recv_sem=in_recv.at[m],
            device_id=device_at(to // 4, y, to % 4, low_z),
            device_id_type=MESH,
        )

    def send_mode(m):
        @pl.when(at_home)
        def _():
            pltpu.make_async_copy(right.at[m, :, columns(group)], start.at[m, rows(sz), :], in_recv.at[m]).start()

        @pl.when(away)
        def _():
            inward(m, 0, in_near.at[m]).start()

        @pl.loop(1, NZ)
        def _(k):
            inward(m, k, in_send.at[m]).start()

    def outward(step, k, send_sem):
        to = (sz + k) % NZ
        return pltpu.make_async_remote_copy(
            src_ref=search.at[step, pl.ds(OFF, M), rows(to), :],
            dst_ref=back.at[step, :, :, columns(group)],
            send_sem=send_sem,
            recv_sem=out_recv.at[step],
            device_id=(block, to),
            device_id_type=MESH,
        )

    def send_near(step):
        @pl.when(at_home)
        def _():
            pltpu.make_async_copy(
                search.at[step, pl.ds(OFF, M), rows(sz), :], back.at[step, :, :, columns(group)], out_recv.at[step]
            ).start()

        @pl.when(away)
        def _():
            outward(step, 0, out_near.at[step]).start()

    def send_share(step, stage):
        begin = 1 + sum(PACE[step][:stage])

        @pl.loop(begin, begin + PACE[step][stage])
        def _(k):
            outward(step, k, out_send.at[step]).start()

    def send_one(step, stage, m):
        begin = 1 + sum(PACE[step][:stage])

        @pl.when(m < PACE[step][stage])
        def _():
            outward(step, begin + m, out_send.at[step]).start()

    def halo_down(step, m):
        return pltpu.make_async_remote_copy(
            src_ref=search.at[step, OFF + m],
            dst_ref=search.at[step, OFF + M + m],
            send_sem=halo_send.at[step, m],
            recv_sem=halo_recv.at[step, m],
            device_id=down,
            device_id_type=MESH,
        )

    def halo_up(step, m):
        return pltpu.make_async_remote_copy(
            src_ref=search.at[step, OFF + m],
            dst_ref=search.at[step, m - (M - OFF)],
            send_sem=halo_send.at[step, m + M - OFF],
            recv_sem=halo_recv.at[step, m + M - OFF],
            device_id=up,
            device_id_type=MESH,
        )

    def send_halo(step, m):
        @pl.when(m < OFF)
        def _():
            halo_down(step, m).start()

        @pl.when(m >= M - OFF)
        def _():
            halo_up(step, m).start()

    for m in range(WINDOW):
        send_mode((m + 3) % M)

    sizes_down = jnp.transpose(jnp.broadcast_to(sizes[...], (NC, NC)))

    @pl.loop(0, M)
    def _(m):
        factor[m] = -1.0 / (sizes_down + wave_row(block, m, group))

    def precondition(step, m, rounded):
        spectral = jnp.dot(inverse[...], rounded, preferred_element_type=jnp.float32)
        scaled = (spectral * factor[m]).astype(jnp.bfloat16)
        result = jnp.dot(basis[...], scaled, preferred_element_type=jnp.float32)
        search[step, OFF + m] = result.astype(jnp.bfloat16)

    def apply(step):
        @pl.loop(0, OFF)
        def _(m):
            halo_down(step, m).wait_recv()
            halo_up(step, m + M - OFF).wait_recv()

        sums[...] = jnp.zeros_like(sums)

        @pl.loop(0, M)
        def _(m):
            send_one(step, 1, m)
            total = -wave_row(block, m, group) * search[step, OFF + m].astype(jnp.float32)
            for h in range(H):
                total = total + jnp.dot(
                    blocks[m, h], search[step, OFF + m + offsets[h]], preferred_element_type=jnp.float32
                )
            if step == 0:
                image[m] = total
                before = start[m]
            else:
                before = residual[m]
            sums[0] += jnp.sum((total * before).reshape(NC // 8, 8, COLS), axis=0)
            sums[1] += jnp.sum((total * total).reshape(NC // 8, 8, COLS), axis=0)

    def row_copy(step, k):
        to = (sz + k) % NZ
        return pltpu.make_async_remote_copy(
            src_ref=parts.at[step],
            dst_ref=row_sums.at[step, sz],
            send_sem=row_send.at[step, k],
            recv_sem=row_recv.at[step, k],
            device_id=(sx, to),
            device_id_type=MESH,
        )

    def all_copy(step, k):
        to = (sx + k) % NX
        return pltpu.make_async_remote_copy(
            src_ref=row_total.at[step],
            dst_ref=all_sums.at[step, sx],
            send_sem=all_send.at[step, k],
            recv_sem=all_recv.at[step, k],
            device_id=(to, sz),
            device_id_type=MESH,
        )

    first_half = lax.broadcasted_iota(jnp.int32, (8, 128), 1) < 64

    def step_size(step):
        def fold(value):
            value = value[:, :128] + value[:, 128:]
            value = value + pltpu.roll(value, 64, 1)
            return value + pltpu.roll(value, 32, 1)

        both = jnp.where(first_half, fold(sums[0]), fold(sums[1]))
        mine = jnp.sum(both, axis=0, keepdims=True)
        parts[step] = mine
        row_sums[step, sz] = mine

        @pl.loop(1, NZ)
        def _(k):
            row_copy(step, k).start()

        send_share(step, 2)

        @pl.loop(1, NZ)
        def _(k):
            row_copy(step, k).wait_recv()

        of_row = row_sums[step, 0]
        for index in range(1, NZ):
            of_row = of_row + row_sums[step, index]
        row_total[step] = of_row
        all_sums[step, sx] = of_row

        @pl.loop(1, NX)
        def _(k):
            all_copy(step, k).start()

        send_share(step, 3)

        @pl.loop(1, NX)
        def _(k):
            all_copy(step, k).wait_recv()

        of_all = all_sums[step, 0]
        for index in range(1, NX):
            of_all = of_all + all_sums[step, index]
        of_all = jnp.broadcast_to(of_all, (8, 128))
        swapped = pltpu.roll(of_all, 64, 1)
        aligned = jnp.where(first_half, of_all, swapped)
        energy = jnp.where(first_half, swapped, of_all)
        return (aligned / (energy + 1e-6))[0:1]

    def first_modes(begin, end):
        @pl.loop(begin, end)
        def _(turn):
            m = (turn + 3) % M
            pltpu.make_async_copy(start.at[m], start.at[m], in_recv.at[m]).wait()

            @pl.when(turn + WINDOW < M)
            def _():
                send_mode((turn + WINDOW + 3) % M)

            precondition(0, m, start[m].astype(jnp.bfloat16))
            send_halo(0, m)

    first_modes(0, PASS_AFTER)

    @pl.when(away)
    def _():
        for side in range(2):
            arrived(2 * (x % 2) + side).wait()
            forward(side).start()

    first_modes(PASS_AFTER, M)
    send_near(0)
    send_share(0, 0)

    @pl.when(at_home)
    def _():
        load_blocks.wait()

    @pl.when(away)
    def _():
        for side in range(2):
            arrived(2 * (1 - x % 2) + side).wait()

    apply(0)
    first = step_size(0)
    first_wide = jnp.concatenate([first, first], axis=1)

    @pl.loop(0, M)
    def _(turn):
        m = (turn + 3) % M
        send_one(0, 4, turn)
        left = start[m] - first_wide * image[m]
        residual[m] = left
        precondition(1, m, left.astype(jnp.bfloat16))
        send_halo(1, m)

    send_near(1)
    send_share(1, 0)
    apply(1)
    second = step_size(1)

    for step in range(2):
        pltpu.make_async_copy(back.at[step], back.at[step], out_recv.at[step]).wait()

    reach = KZ * R // 128
    first_all = jnp.tile(first, (1, reach))
    second_all = jnp.tile(second, (1, reach))

    @pl.loop(0, M)
    def _(m):
        final[m] = first_all * back[0, m].astype(jnp.float32) + second_all * back[1, m].astype(jnp.float32)
        pltpu.make_async_copy(final.at[m], out.at[m], final_sem.at[m]).start()

    @pl.loop(0, M)
    def _(m):
        part = start.at[m, pl.ds(0, NC - ROWS), :]
        pltpu.make_async_copy(part, part, in_send.at[m]).wait()

    for step in range(2):
        part = search.at[step, pl.ds(OFF, M), pl.ds(0, NC - ROWS), :]
        pltpu.make_async_copy(part, part, out_send.at[step]).wait()

    @pl.when(at_home)
    def _():
        for side in range(2):
            push(side).wait_send()

    @pl.when(away)
    def _():
        @pl.loop(0, M)
        def _(m):
            inward(m, 0, in_near.at[m]).wait_send()

        for step in range(2):
            outward(step, 0, out_near.at[step]).wait_send()
        for side in range(2):
            forward(side).wait_send()

    for step in range(2):

        @pl.loop(1, NZ)
        def _(k):
            row_copy(step, k).wait_send()

        @pl.loop(1, NX)
        def _(k):
            all_copy(step, k).wait_send()

        @pl.loop(0, OFF)
        def _(m):
            halo_down(step, m).wait_send()
            halo_up(step, m + M - OFF).wait_send()

    @pl.loop(0, M)
    def _(m):
        pltpu.make_async_copy(final.at[m], out.at[m], final_sem.at[m]).wait()


PASS_AFTER = 5


def shards(right_side, coupling, harmonic_offsets, eigen_basis, eigen_inverse, eigen_size):
    vmem = pl.BlockSpec(memory_space=pltpu.VMEM)
    anywhere = pl.BlockSpec(memory_space=pl.ANY)
    low, full = jnp.bfloat16, jnp.float32
    dma = pltpu.SemaphoreType.DMA
    return pl.pallas_call(
        kernel,
        out_shape=jax.ShapeDtypeStruct((M, ROWS, KZ * R), full),
        in_specs=[pl.BlockSpec(memory_space=pltpu.SMEM), anywhere, anywhere, vmem, vmem, vmem],
        out_specs=anywhere,
        scratch_shapes=[
            pltpu.VMEM((M, NC, COLS), full),
            pltpu.VMEM((M, NC, COLS), full),
            pltpu.VMEM((M, NC, COLS), full),
            pltpu.VMEM((M, NC, COLS), full),
            pltpu.VMEM((M, H, NC, NC), low),
            pltpu.VMEM((2, M + 2 * OFF, NC, COLS), low),
            pltpu.VMEM((2, M, ROWS, KZ * R), low),
            pltpu.VMEM((M, ROWS, KZ * R), full),
            pltpu.VMEM((2, 8, COLS), full),
            pltpu.VMEM((2, 1, 128), full),
            pltpu.VMEM((2, NZ, 1, 128), full),
            pltpu.VMEM((2, 1, 128), full),
            pltpu.VMEM((2, NX, 1, 128), full),
            dma((1,)),
            dma((M,)),
            dma((M,)),
            dma((M,)),
            dma((2,)),
            dma((2,)),
            dma((2,)),
            dma((2, 2 * OFF)),
            dma((2, 2 * OFF)),
            dma((2,)),
            dma((4,)),
            dma((2,)),
            dma((2, NZ)),
            dma((2, NZ)),
            dma((2, NX)),
            dma((2, NX)),
            dma((M,)),
        ],
        compiler_params=pltpu.CompilerParams(
            collective_id=0, has_side_effects=True, vmem_limit_bytes=56 * 2**20
        ),
    )(harmonic_offsets, right_side, coupling, eigen_basis, eigen_inverse, eigen_size.reshape(1, NC))


def solution(mesh):
    in_specs = (P("sx", "sz", None), P("sx", None, None, None), P(), P(), P(), P())
    out_specs = P("sx", "sz", None)
    return jax.shard_map(shards, mesh=mesh, in_specs=in_specs, out_specs=out_specs, check_vma=False)
```

```python
import jax
import jax.numpy as jnp
from jax import lax
from jax.experimental import pallas as pl
from jax.experimental.pallas import tpu as pltpu
from jax.sharding import PartitionSpec as P

KX = 72
KZ = 128
NC = 256
H = 5
OFF = 6
R = 32
NX = 8
NZ = 16
M = KX // NX
ROWS = NC // NZ
COLS = KZ * R // NZ
SPANS = KZ // NZ
QUARTER = NC // 4
MESH = pl.DeviceIdType.MESH
WINDOW = 4
LAG = 1
PACE = ((0, 2, 4, 4, 5), (8, 0, 4, 3, 0))


def device_at(x, y, z, core):
    return 2 * y + z % 2, 4 * x + 2 * (z // 2) + core


def wave_row(block, mode, group):
    index = block * M + mode
    signed_x = jnp.where(index < KX // 2, index, index - KX).astype(jnp.float32) * (4.0 / KX)
    column = lax.broadcasted_iota(jnp.int32, (1, COLS), 1)
    span = group * SPANS + column // R
    signed_z = jnp.where(span < KZ // 2, span, span - KZ).astype(jnp.float32) * (4.0 / KZ)
    return 1.0 + signed_x * signed_x + signed_z * signed_z


def kernel(
    offsets, right, coupling, basis, inverse, sizes, out,
    start, factor, image, residual, blocks,
    search, back, final, sums, parts, row_sums, row_total, all_sums,
    load_sem, in_send, in_near, in_recv, out_send, out_near, out_recv, halo_send, halo_recv,
    block_send, block_recv, pass_send, row_send, row_recv, all_send, all_recv, final_sem,
):
    sx, sz = lax.axis_index("sx"), lax.axis_index("sz")
    y, low_z = sx // 2, sx % 2
    x, core = sz // 4, sz % 2
    z = 2 * ((sz // 2) % 2) + low_z
    block = 2 * y + core
    group = 4 * x + z
    at_home = core == low_z
    away = core != low_z
    other = sz + 1 - 2 * core
    up = ((sx + 2 * core) % NX, other)
    down = ((sx + NX - 2 * (1 - core)) % NX, other)
    across = ((sx + NX + 4 * core - 2) % NX, other)

    load_blocks = pltpu.make_async_copy(coupling, blocks, load_sem.at[0])

    @pl.when(at_home)
    def _():
        load_blocks.start()

    barrier = pltpu.get_barrier_semaphore()

    place = NZ * low_z + sz

    @pl.loop(1, 2 * NZ)
    def _(k):
        to = (place + k) % (2 * NZ)
        pl.semaphore_signal(barrier, inc=1, device_id=(2 * y + to // NZ, to % NZ), device_id_type=MESH)

    @pl.loop(1, NX)
    def _(k):
        pl.semaphore_signal(barrier, inc=1, device_id=((sx + k) % NX, sz), device_id_type=MESH)

    pl.semaphore_signal(barrier, inc=1, device_id=across, device_id_type=MESH)
    pl.semaphore_wait(barrier, 2 * NZ - 1 + NX - 1 + 1)

    def columns(index):
        return pl.ds(pl.multiple_of(index * COLS, COLS), COLS)

    def rows(index):
        return pl.ds(pl.multiple_of(index * ROWS, ROWS), ROWS)

    def quarter(index):
        return pl.ds(pl.multiple_of(index * QUARTER, QUARTER), QUARTER)

    def push(m, side):
        index = 2 * (x % 2) + side
        return pltpu.make_async_remote_copy(
            src_ref=coupling.at[m, :, quarter(index), :],
            dst_ref=blocks.at[m, :, quarter(index), :],
            send_sem=block_send.at[m, side],
            recv_sem=block_recv.at[m, index],
            device_id=device_at(x, y, (z + 1 + 2 * side) % 4, core),
            device_id_type=MESH,
        )

    def forward(m, side):
        index = 2 * (x % 2) + side
        return pltpu.make_async_remote_copy(
            src_ref=blocks.at[m, :, quarter(index), :],
            dst_ref=blocks.at[m, :, quarter(index), :],
            send_sem=pass_send.at[m, side],
            recv_sem=block_recv.at[m, index],
            device_id=(sx, (sz + 4 + 8 * side) % NZ),
            device_id_type=MESH,
        )

    def arrived(m, index):
        part = blocks.at[m, :, quarter(index), :]
        return pltpu.make_async_copy(part, part, block_recv.at[m, index])

    def pass_on(m):
        @pl.when(away)
        def _():
            for side in range(2):
                arrived(m, 2 * (x % 2) + side).wait()
                forward(m, side).start()

    def inward(m, k, send_sem):
        to = (group + k) % NZ
        return pltpu.make_async_remote_copy(
            src_ref=right.at[m, :, columns(to)],
            dst_ref=start.at[m, rows(sz), :],
            send_sem=send_sem,
            recv_sem=in_recv.at[m],
            device_id=device_at(to // 4, y, to % 4, low_z),
            device_id_type=MESH,
        )

    def send_mode(turn):
        m = (turn + 3) % M

        @pl.when(at_home)
        def _():
            for side in range(2):
                push(turn, side).start()

            pltpu.make_async_copy(right.at[m, :, columns(group)], start.at[m, rows(sz), :], in_recv.at[m]).start()

        @pl.when(away)
        def _():
            inward(m, 0, in_near.at[m]).start()

        @pl.loop(1, NZ)
        def _(k):
            inward(m, k, in_send.at[m]).start()

    def outward(step, k, send_sem):
        to = (sz + k) % NZ
        return pltpu.make_async_remote_copy(
            src_ref=search.at[step, pl.ds(OFF, M), rows(to), :],
            dst_ref=back.at[step, :, :, columns(group)],
            send_sem=send_sem,
            recv_sem=out_recv.at[step],
            device_id=(block, to),
            device_id_type=MESH,
        )

    def send_near(step):
        @pl.when(at_home)
        def _():
            pltpu.make_async_copy(
                search.at[step, pl.ds(OFF, M), rows(sz), :], back.at[step, :, :, columns(group)], out_recv.at[step]
            ).start()

        @pl.when(away)
        def _():
            outward(step, 0, out_near.at[step]).start()

    def send_share(step, stage):
        begin = 1 + sum(PACE[step][:stage])

        @pl.loop(begin, begin + PACE[step][stage])
        def _(k):
            outward(step, k, out_send.at[step]).start()

    def send_one(step, stage, m):
        begin = 1 + sum(PACE[step][:stage])

        @pl.when(m < PACE[step][stage])
        def _():
            outward(step, begin + m, out_send.at[step]).start()

    def halo_down(step, m):
        return pltpu.make_async_remote_copy(
            src_ref=search.at[step, OFF + m],
            dst_ref=search.at[step, OFF + M + m],
            send_sem=halo_send.at[step, m],
            recv_sem=halo_recv.at[step, m],
            device_id=down,
            device_id_type=MESH,
        )

    def halo_up(step, m):
        return pltpu.make_async_remote_copy(
            src_ref=search.at[step, OFF + m],
            dst_ref=search.at[step, m - (M - OFF)],
            send_sem=halo_send.at[step, m + M - OFF],
            recv_sem=halo_recv.at[step, m + M - OFF],
            device_id=up,
            device_id_type=MESH,
        )

    def send_halo(step, m):
        @pl.when(m < OFF)
        def _():
            halo_down(step, m).start()

        @pl.when(m >= M - OFF)
        def _():
            halo_up(step, m).start()

    for m in range(WINDOW):
        send_mode(m)

    sizes_down = jnp.transpose(jnp.broadcast_to(sizes[...], (NC, NC)))

    @pl.loop(0, M)
    def _(m):
        factor[m] = -1.0 / (sizes_down + wave_row(block, m, group))

    def precondition(step, m, rounded):
        spectral = jnp.dot(inverse[...], rounded, preferred_element_type=jnp.float32)
        scaled = (spectral * factor[m]).astype(jnp.bfloat16)
        result = jnp.dot(basis[...], scaled, preferred_element_type=jnp.float32)
        search[step, OFF + m] = result.astype(jnp.bfloat16)

    def apply(step):
        @pl.loop(0, OFF)
        def _(m):
            halo_down(step, m).wait_recv()
            halo_up(step, m + M - OFF).wait_recv()

        sums[...] = jnp.zeros_like(sums)

        @pl.loop(0, M)
        def _(m):
            if step == 0:

                @pl.when(away)
                def _():
                    for side in range(2):
                        arrived(m, 2 * (1 - x % 2) + side).wait()

            send_one(step, 1, m)
            total = -wave_row(block, m, group) * search[step, OFF + m].astype(jnp.float32)
            for h in range(H):
                total = total + jnp.dot(
                    blocks[m, h], search[step, OFF + m + offsets[h]], preferred_element_type=jnp.float32
                )
            if step == 0:
                image[m] = total
                before = start[m]
            else:
                before = residual[m]
            sums[0] += jnp.sum((total * before).reshape(NC // 8, 8, COLS), axis=0)
            sums[1] += jnp.sum((total * total).reshape(NC // 8, 8, COLS), axis=0)

    def row_copy(step, k):
        to = (sz + k) % NZ
        return pltpu.make_async_remote_copy(
            src_ref=parts.at[step],
            dst_ref=row_sums.at[step, sz],
            send_sem=row_send.at[step],
            recv_sem=row_recv.at[step],
            device_id=(sx, to),
            device_id_type=MESH,
        )

    def all_copy(step, k):
        to = (sx + k) % NX
        return pltpu.make_async_remote_copy(
            src_ref=row_total.at[step],
            dst_ref=all_sums.at[step, sx],
            send_sem=all_send.at[step],
            recv_sem=all_recv.at[step],
            device_id=(to, sz),
            device_id_type=MESH,
        )

    first_half = lax.broadcasted_iota(jnp.int32, (8, 128), 1) < 64

    def step_size(step):
        def fold(value):
            value = value[:, :128] + value[:, 128:]
            value = value + pltpu.roll(value, 64, 1)
            return value + pltpu.roll(value, 32, 1)

        both = jnp.where(first_half, fold(sums[0]), fold(sums[1]))
        mine = jnp.sum(both, axis=0, keepdims=True)
        parts[step] = mine
        row_sums[step, sz] = mine

        @pl.loop(1, NZ)
        def _(k):
            row_copy(step, k).start()

        send_share(step, 2)

        others = row_sums.at[step, pl.ds(0, NZ - 1)]
        pltpu.make_async_copy(others, others, row_recv.at[step]).wait()

        of_row = row_sums[step, 0]
        for index in range(1, NZ):
            of_row = of_row + row_sums[step, index]
        row_total[step] = of_row
        all_sums[step, sx] = of_row

        @pl.loop(1, NX)
        def _(k):
            all_copy(step, k).start()

        send_share(step, 3)

        others = all_sums.at[step, pl.ds(0, NX - 1)]
        pltpu.make_async_copy(others, others, all_recv.at[step]).wait()

        of_all = all_sums[step, 0]
        for index in range(1, NX):
            of_all = of_all + all_sums[step, index]
        of_all = jnp.broadcast_to(of_all, (8, 128))
        swapped = pltpu.roll(of_all, 64, 1)
        aligned = jnp.where(first_half, of_all, swapped)
        energy = jnp.where(first_half, swapped, of_all)
        return (aligned / (energy + 1e-6))[0:1]

    def first_modes(begin, end):
        @pl.loop(begin, end)
        def _(turn):
            m = (turn + 3) % M
            pltpu.make_async_copy(start.at[m], start.at[m], in_recv.at[m]).wait()

            @pl.when(turn + WINDOW < M)
            def _():
                send_mode(turn + WINDOW)

            precondition(0, m, start[m].astype(jnp.bfloat16))
            send_halo(0, m)

            @pl.when(turn >= LAG)
            def _():
                pass_on(turn - LAG)

    first_modes(0, M)

    @pl.loop(M - LAG, M)
    def _(m):
        pass_on(m)

    send_near(0)
    send_share(0, 0)

    @pl.when(at_home)
    def _():
        load_blocks.wait()

    apply(0)
    first = step_size(0)
    first_wide = jnp.concatenate([first, first], axis=1)

    @pl.loop(0, M // 3)
    def _(turn):
        modes = [(3 * turn + 3 + each) % M for each in range(3)]
        rounded = []
        for m in modes:
            left = start[m] - first_wide * image[m]
            residual[m] = left
            rounded.append(left.astype(jnp.bfloat16))
        spectral = [jnp.dot(inverse[...], each, preferred_element_type=jnp.float32) for each in rounded]
        scaled = [(each * factor[m]).astype(jnp.bfloat16) for each, m in zip(spectral, modes)]
        for each, m in zip(scaled, modes):
            result = jnp.dot(basis[...], each, preferred_element_type=jnp.float32)
            search[1, OFF + m] = result.astype(jnp.bfloat16)
        for each, m in enumerate(modes):
            send_halo(1, m)
            send_one(0, 4, 3 * turn + each)

    send_near(1)
    send_share(1, 0)
    apply(1)
    second = step_size(1)

    for step in range(2):
        pltpu.make_async_copy(back.at[step], back.at[step], out_recv.at[step]).wait()

    reach = KZ * R // 128
    first_all = jnp.tile(first, (1, reach))
    second_all = jnp.tile(second, (1, reach))

    @pl.loop(0, M)
    def _(m):
        final[m] = first_all * back[0, m].astype(jnp.float32) + second_all * back[1, m].astype(jnp.float32)
        pltpu.make_async_copy(final.at[m], out.at[m], final_sem.at[m]).start()

    @pl.loop(0, M)
    def _(m):
        part = start.at[m, pl.ds(0, NC - ROWS), :]
        pltpu.make_async_copy(part, part, in_send.at[m]).wait()

    for step in range(2):
        part = search.at[step, pl.ds(OFF, M), pl.ds(0, NC - ROWS), :]
        pltpu.make_async_copy(part, part, out_send.at[step]).wait()

    @pl.when(at_home)
    def _():
        @pl.loop(0, M)
        def _(m):
            for side in range(2):
                push(m, side).wait_send()

    @pl.when(away)
    def _():
        @pl.loop(0, M)
        def _(m):
            inward(m, 0, in_near.at[m]).wait_send()
            for side in range(2):
                forward(m, side).wait_send()

        for step in range(2):
            outward(step, 0, out_near.at[step]).wait_send()

    for step in range(2):

        others = row_sums.at[step, pl.ds(0, NZ - 1)]
        pltpu.make_async_copy(others, others, row_send.at[step]).wait()
        others = all_sums.at[step, pl.ds(0, NX - 1)]
        pltpu.make_async_copy(others, others, all_send.at[step]).wait()

        @pl.loop(0, OFF)
        def _(m):
            halo_down(step, m).wait_send()
            halo_up(step, m + M - OFF).wait_send()

    @pl.loop(0, M)
    def _(m):
        pltpu.make_async_copy(final.at[m], out.at[m], final_sem.at[m]).wait()


def shards(right_side, coupling, harmonic_offsets, eigen_basis, eigen_inverse, eigen_size):
    vmem = pl.BlockSpec(memory_space=pltpu.VMEM)
    anywhere = pl.BlockSpec(memory_space=pl.ANY)
    low, full = jnp.bfloat16, jnp.float32
    dma = pltpu.SemaphoreType.DMA
    return pl.pallas_call(
        kernel,
        out_shape=jax.ShapeDtypeStruct((M, ROWS, KZ * R), full),
        in_specs=[pl.BlockSpec(memory_space=pltpu.SMEM), anywhere, anywhere, vmem, vmem, vmem],
        out_specs=anywhere,
        scratch_shapes=[
            pltpu.VMEM((M, NC, COLS), full),
            pltpu.VMEM((M, NC, COLS), full),
            pltpu.VMEM((M, NC, COLS), full),
            pltpu.VMEM((M, NC, COLS), full),
            pltpu.VMEM((M, H, NC, NC), low),
            pltpu.VMEM((2, M + 2 * OFF, NC, COLS), low),
            pltpu.VMEM((2, M, ROWS, KZ * R), low),
            pltpu.VMEM((M, ROWS, KZ * R), full),
            pltpu.VMEM((2, 8, COLS), full),
            pltpu.VMEM((2, 1, 128), full),
            pltpu.VMEM((2, NZ, 1, 128), full),
            pltpu.VMEM((2, 1, 128), full),
            pltpu.VMEM((2, NX, 1, 128), full),
            dma((1,)),
            dma((M,)),
            dma((M,)),
            dma((M,)),
            dma((2,)),
            dma((2,)),
            dma((2,)),
            dma((2, 2 * OFF)),
            dma((2, 2 * OFF)),
            dma((M, 2)),
            dma((M, 4)),
            dma((M, 2)),
            dma((2,)),
            dma((2,)),
            dma((2,)),
            dma((2,)),
            dma((M,)),
        ],
        compiler_params=pltpu.CompilerParams(
            collective_id=0, has_side_effects=True, vmem_limit_bytes=56 * 2**20
        ),
    )(harmonic_offsets, right_side, coupling, eigen_basis, eigen_inverse, eigen_size.reshape(1, NC))


def solution(mesh):
    in_specs = (P("sx", "sz", None), P("sx", None, None, None), P(), P(), P(), P())
    out_specs = P("sx", "sz", None)
    return jax.shard_map(shards, mesh=mesh, in_specs=in_specs, out_specs=out_specs, check_vma=False)
```

```python
import jax
import jax.numpy as jnp
from jax import lax
from jax.experimental import pallas as pl
from jax.experimental.pallas import tpu as pltpu
from jax.sharding import PartitionSpec as P

KX = 72
KZ = 128
NC = 256
H = 5
OFF = 6
R = 32
NX = 8
NZ = 16
M = KX // NX
ROWS = NC // NZ
COLS = KZ * R // NZ
SPANS = KZ // NZ
QUARTER = NC // 4
MESH = pl.DeviceIdType.MESH
WINDOW = 4
LATE = 0
LAG = 0
PACE = ((0, 2, 4, 4, 5), (8, 0, 4, 3, 0))


def device_at(x, y, z, core):
    return 2 * y + z % 2, 4 * x + 2 * (z // 2) + core


def wave_row(block, mode, group):
    index = block * M + mode
    signed_x = jnp.where(index < KX // 2, index, index - KX).astype(jnp.float32) * (4.0 / KX)
    column = lax.broadcasted_iota(jnp.int32, (1, COLS), 1)
    span = group * SPANS + column // R
    signed_z = jnp.where(span < KZ // 2, span, span - KZ).astype(jnp.float32) * (4.0 / KZ)
    return 1.0 + signed_x * signed_x + signed_z * signed_z


def kernel(
    offsets, right, coupling, basis, inverse, sizes, back, steps,
    start, factor, image, residual, blocks,
    search, sums, parts, row_sums, row_total, all_sums,
    load_sem, in_send, in_near, in_recv, out_send, out_near, out_recv, halo_send, halo_recv,
    block_send, block_recv, pass_send, row_send, row_recv, all_send, all_recv,
):
    sx, sz = lax.axis_index("sx"), lax.axis_index("sz")
    y, low_z = sx // 2, sx % 2
    x, core = sz // 4, sz % 2
    z = 2 * ((sz // 2) % 2) + low_z
    block = 2 * y + core
    group = 4 * x + z
    at_home = core == low_z
    away = core != low_z
    other = sz + 1 - 2 * core
    up = ((sx + 2 * core) % NX, other)
    down = ((sx + NX - 2 * (1 - core)) % NX, other)
    across = ((sx + NX + 4 * core - 2) % NX, other)

    load_blocks = pltpu.make_async_copy(coupling, blocks, load_sem.at[0])

    @pl.when(at_home)
    def _():
        load_blocks.start()

    barrier = pltpu.get_barrier_semaphore()

    place = NZ * low_z + sz

    @pl.loop(1, 2 * NZ)
    def _(k):
        to = (place + k) % (2 * NZ)
        pl.semaphore_signal(barrier, inc=1, device_id=(2 * y + to // NZ, to % NZ), device_id_type=MESH)

    @pl.loop(1, NX)
    def _(k):
        pl.semaphore_signal(barrier, inc=1, device_id=((sx + k) % NX, sz), device_id_type=MESH)

    pl.semaphore_signal(barrier, inc=1, device_id=across, device_id_type=MESH)
    pl.semaphore_wait(barrier, 2 * NZ - 1 + NX - 1 + 1)

    def columns(index):
        return pl.ds(pl.multiple_of(index * COLS, COLS), COLS)

    def rows(index):
        return pl.ds(pl.multiple_of(index * ROWS, ROWS), ROWS)

    def quarter(index):
        return pl.ds(pl.multiple_of(index * QUARTER, QUARTER), QUARTER)

    def push(m, side):
        index = 2 * (x % 2) + side
        return pltpu.make_async_remote_copy(
            src_ref=coupling.at[m, :, quarter(index), :],
            dst_ref=blocks.at[m, :, quarter(index), :],
            send_sem=block_send.at[m, side],
            recv_sem=block_recv.at[m, index],
            device_id=device_at(x, y, (z + 1 + 2 * side) % 4, core),
            device_id_type=MESH,
        )

    def forward(m, side):
        index = 2 * (x % 2) + side
        return pltpu.make_async_remote_copy(
            src_ref=blocks.at[m, :, quarter(index), :],
            dst_ref=blocks.at[m, :, quarter(index), :],
            send_sem=pass_send.at[m, side],
            recv_sem=block_recv.at[m, index],
            device_id=(sx, (sz + 4 + 8 * side) % NZ),
            device_id_type=MESH,
        )

    def arrived(m, index):
        part = blocks.at[m, :, quarter(index), :]
        return pltpu.make_async_copy(part, part, block_recv.at[m, index])

    def pass_on(m):
        @pl.when(away)
        def _():
            for side in range(2):
                arrived(m, 2 * (x % 2) + side).wait()
                forward(m, side).start()

    def inward(m, k, send_sem):
        to = (group + k) % NZ
        return pltpu.make_async_remote_copy(
            src_ref=right.at[m, :, columns(to)],
            dst_ref=start.at[m, rows(sz), :],
            send_sem=send_sem,
            recv_sem=in_recv.at[m],
            device_id=device_at(to // 4, y, to % 4, low_z),
            device_id_type=MESH,
        )

    def send_mode(turn):
        m = (turn + 3) % M

        @pl.when(at_home)
        def _():
            pltpu.make_async_copy(right.at[m, :, columns(group)], start.at[m, rows(sz), :], in_recv.at[m]).start()

        @pl.when(away)
        def _():
            inward(m, 0, in_near.at[m]).start()

        @pl.loop(1, NZ)
        def _(k):
            inward(m, k, in_send.at[m]).start()

        @pl.when(at_home & (turn >= LATE))
        def _():
            for side in range(2):
                push(turn - LATE, side).start()

    def outward(step, k, send_sem):
        to = (sz + k) % NZ
        return pltpu.make_async_remote_copy(
            src_ref=search.at[step, pl.ds(OFF, M), rows(to), :],
            dst_ref=back.at[step, :, :, columns(group)],
            send_sem=send_sem,
            recv_sem=out_recv.at[step],
            device_id=(block, to),
            device_id_type=MESH,
        )

    def send_near(step):
        @pl.when(at_home)
        def _():
            pltpu.make_async_copy(
                search.at[step, pl.ds(OFF, M), rows(sz), :], back.at[step, :, :, columns(group)], out_recv.at[step]
            ).start()

        @pl.when(away)
        def _():
            outward(step, 0, out_near.at[step]).start()

    def send_share(step, stage):
        begin = 1 + sum(PACE[step][:stage])

        @pl.loop(begin, begin + PACE[step][stage])
        def _(k):
            outward(step, k, out_send.at[step]).start()

    def send_one(step, stage, m):
        begin = 1 + sum(PACE[step][:stage])

        @pl.when(m < PACE[step][stage])
        def _():
            outward(step, begin + m, out_send.at[step]).start()

    def halo_down(step, m):
        return pltpu.make_async_remote_copy(
            src_ref=search.at[step, OFF + m],
            dst_ref=search.at[step, OFF + M + m],
            send_sem=halo_send.at[step, m],
            recv_sem=halo_recv.at[step, m],
            device_id=down,
            device_id_type=MESH,
        )

    def halo_up(step, m):
        return pltpu.make_async_remote_copy(
            src_ref=search.at[step, OFF + m],
            dst_ref=search.at[step, m - (M - OFF)],
            send_sem=halo_send.at[step, m + M - OFF],
            recv_sem=halo_recv.at[step, m + M - OFF],
            device_id=up,
            device_id_type=MESH,
        )

    def send_halo(step, m):
        @pl.when(m < OFF)
        def _():
            halo_down(step, m).start()

        @pl.when(m >= M - OFF)
        def _():
            halo_up(step, m).start()

    for m in range(WINDOW):
        send_mode(m)

    sizes_down = jnp.transpose(jnp.broadcast_to(sizes[...], (NC, NC)))

    @pl.loop(0, M)
    def _(m):
        factor[m] = -1.0 / (sizes_down + wave_row(block, m, group))

    def precondition(step, m, rounded):
        spectral = jnp.dot(inverse[...], rounded, preferred_element_type=jnp.float32)
        scaled = (spectral * factor[m]).astype(jnp.bfloat16)
        result = jnp.dot(basis[...], scaled, preferred_element_type=jnp.float32)
        search[step, OFF + m] = result.astype(jnp.bfloat16)

    def apply(step):
        @pl.loop(0, OFF)
        def _(m):
            halo_down(step, m).wait_recv()
            halo_up(step, m + M - OFF).wait_recv()

        sums[...] = jnp.zeros_like(sums)

        def one(m):
            total = -wave_row(block, m, group) * search[step, OFF + m].astype(jnp.float32)
            for h in range(H):
                total = total + jnp.dot(
                    blocks[m, h], search[step, OFF + m + offsets[h]], preferred_element_type=jnp.float32
                )
            if step == 0:
                image[m] = total
                before = start[m]
            else:
                before = residual[m]
            sums[0] += jnp.sum((total * before).reshape(NC // 8, 8, COLS), axis=0)
            sums[1] += jnp.sum((total * total).reshape(NC // 8, 8, COLS), axis=0)

        @pl.loop(0, M // 3)
        def _(turn):
            modes = [3 * turn + each for each in range(3)]
            if step == 0:

                @pl.when(away)
                def _():
                    for m in modes:
                        for side in range(2):
                            arrived(m, 2 * (1 - x % 2) + side).wait()

            for m in modes:
                send_one(step, 1, m)
            for m in modes:
                one(m)

    def row_copy(step, k):
        to = (sz + k) % NZ
        return pltpu.make_async_remote_copy(
            src_ref=parts.at[step],
            dst_ref=row_sums.at[step, sz],
            send_sem=row_send.at[step],
            recv_sem=row_recv.at[step],
            device_id=(sx, to),
            device_id_type=MESH,
        )

    def all_copy(step, k):
        to = (sx + k) % NX
        return pltpu.make_async_remote_copy(
            src_ref=row_total.at[step],
            dst_ref=all_sums.at[step, sx],
            send_sem=all_send.at[step],
            recv_sem=all_recv.at[step],
            device_id=(to, sz),
            device_id_type=MESH,
        )

    first_half = lax.broadcasted_iota(jnp.int32, (8, 128), 1) < 64

    def step_size(step):
        def fold(value):
            value = value[:, :128] + value[:, 128:]
            value = value + pltpu.roll(value, 64, 1)
            return value + pltpu.roll(value, 32, 1)

        both = jnp.where(first_half, fold(sums[0]), fold(sums[1]))
        mine = jnp.sum(both, axis=0, keepdims=True)
        parts[step] = mine
        row_sums[step, sz] = mine

        @pl.loop(1, NZ)
        def _(k):
            row_copy(step, k).start()

        send_share(step, 2)

        others = row_sums.at[step, pl.ds(0, NZ - 1)]
        pltpu.make_async_copy(others, others, row_recv.at[step]).wait()

        of_row = row_sums[step, 0]
        for index in range(1, NZ):
            of_row = of_row + row_sums[step, index]
        row_total[step] = of_row
        all_sums[step, sx] = of_row

        @pl.loop(1, NX)
        def _(k):
            all_copy(step, k).start()

        send_share(step, 3)

        others = all_sums.at[step, pl.ds(0, NX - 1)]
        pltpu.make_async_copy(others, others, all_recv.at[step]).wait()

        of_all = all_sums[step, 0]
        for index in range(1, NX):
            of_all = of_all + all_sums[step, index]
        of_all = jnp.broadcast_to(of_all, (8, 128))
        swapped = pltpu.roll(of_all, 64, 1)
        aligned = jnp.where(first_half, of_all, swapped)
        energy = jnp.where(first_half, swapped, of_all)
        return (aligned / (energy + 1e-6))[0:1]

    def first_modes(begin, end):
        @pl.loop(begin, end)
        def _(turn):
            m = (turn + 3) % M
            pltpu.make_async_copy(start.at[m], start.at[m], in_recv.at[m]).wait()

            @pl.when(turn + WINDOW < M)
            def _():
                send_mode(turn + WINDOW)

            precondition(0, m, start[m].astype(jnp.bfloat16))
            send_halo(0, m)

            @pl.when(turn >= LAG)
            def _():
                pass_on(turn - LAG)

    first_modes(0, M)

    @pl.loop(M - LAG, M)
    def _(m):
        pass_on(m)

    send_near(0)
    send_share(0, 0)

    @pl.when(at_home)
    def _():
        load_blocks.wait()

    apply(0)
    first = step_size(0)
    first_wide = jnp.concatenate([first, first], axis=1)

    @pl.loop(0, M // 3)
    def _(turn):
        modes = [(3 * turn + 3 + each) % M for each in range(3)]
        rounded = []
        for m in modes:
            left = start[m] - first_wide * image[m]
            residual[m] = left
            rounded.append(left.astype(jnp.bfloat16))
        spectral = [jnp.dot(inverse[...], each, preferred_element_type=jnp.float32) for each in rounded]
        scaled = [(each * factor[m]).astype(jnp.bfloat16) for each, m in zip(spectral, modes)]
        for each, m in zip(scaled, modes):
            result = jnp.dot(basis[...], each, preferred_element_type=jnp.float32)
            search[1, OFF + m] = result.astype(jnp.bfloat16)
        for each, m in enumerate(modes):
            send_halo(1, m)
            send_one(0, 4, 3 * turn + each)

    send_near(1)
    send_share(1, 0)
    apply(1)
    second = step_size(1)

    for step in range(2):
        pltpu.make_async_copy(back.at[step], back.at[step], out_recv.at[step]).wait()

    steps[0:1, :] = first
    steps[1:2, :] = second

    @pl.loop(0, M)
    def _(m):
        part = start.at[m, pl.ds(0, NC - ROWS), :]
        pltpu.make_async_copy(part, part, in_send.at[m]).wait()

    for step in range(2):
        part = search.at[step, pl.ds(OFF, M), pl.ds(0, NC - ROWS), :]
        pltpu.make_async_copy(part, part, out_send.at[step]).wait()

    @pl.when(at_home)
    def _():
        @pl.loop(0, M)
        def _(m):
            for side in range(2):
                push(m, side).wait_send()

    @pl.when(away)
    def _():
        @pl.loop(0, M)
        def _(m):
            inward(m, 0, in_near.at[m]).wait_send()
            for side in range(2):
                forward(m, side).wait_send()

        for step in range(2):
            outward(step, 0, out_near.at[step]).wait_send()

    for step in range(2):

        others = row_sums.at[step, pl.ds(0, NZ - 1)]
        pltpu.make_async_copy(others, others, row_send.at[step]).wait()
        others = all_sums.at[step, pl.ds(0, NX - 1)]
        pltpu.make_async_copy(others, others, all_send.at[step]).wait()

        @pl.loop(0, OFF)
        def _(m):
            halo_down(step, m).wait_send()
            halo_up(step, m + M - OFF).wait_send()


def combine(steps, back, out, first, second, total, in_sem, out_sem):
    def fetch(m, step, into):
        return pltpu.make_async_copy(back.at[step, m], into.at[m], in_sem.at[step, m])

    def store(m):
        return pltpu.make_async_copy(total.at[m], out.at[m], out_sem.at[m])

    @pl.loop(0, M)
    def _(m):
        fetch(m, 0, first).start()
        fetch(m, 1, second).start()

    wide = jnp.tile(steps[...], (1, KZ * R // 128))

    @pl.loop(0, M)
    def _(m):
        fetch(m, 0, first).wait()
        fetch(m, 1, second).wait()
        total[m] = wide[0:1] * first[m].astype(jnp.float32) + wide[1:2] * second[m].astype(jnp.float32)
        store(m).start()

    @pl.loop(0, M)
    def _(m):
        store(m).wait()


def shards(right_side, coupling, harmonic_offsets, eigen_basis, eigen_inverse, eigen_size):
    vmem = pl.BlockSpec(memory_space=pltpu.VMEM)
    anywhere = pl.BlockSpec(memory_space=pl.ANY)
    low, full = jnp.bfloat16, jnp.float32
    dma = pltpu.SemaphoreType.DMA
    back, steps = pl.pallas_call(
        kernel,
        out_shape=(jax.ShapeDtypeStruct((2, M, ROWS, KZ * R), low), jax.ShapeDtypeStruct((2, 128), full)),
        in_specs=[pl.BlockSpec(memory_space=pltpu.SMEM), anywhere, anywhere, vmem, vmem, vmem],
        out_specs=(anywhere, vmem),
        scratch_shapes=[
            pltpu.VMEM((M, NC, COLS), full),
            pltpu.VMEM((M, NC, COLS), full),
            pltpu.VMEM((M, NC, COLS), full),
            pltpu.VMEM((M, NC, COLS), full),
            pltpu.VMEM((M, H, NC, NC), low),
            pltpu.VMEM((2, M + 2 * OFF, NC, COLS), low),
            pltpu.VMEM((2, 8, COLS), full),
            pltpu.VMEM((2, 1, 128), full),
            pltpu.VMEM((2, NZ, 1, 128), full),
            pltpu.VMEM((2, 1, 128), full),
            pltpu.VMEM((2, NX, 1, 128), full),
            dma((1,)),
            dma((M,)),
            dma((M,)),
            dma((M,)),
            dma((2,)),
            dma((2,)),
            dma((2,)),
            dma((2, 2 * OFF)),
            dma((2, 2 * OFF)),
            dma((M, 2)),
            dma((M, 4)),
            dma((M, 2)),
            dma((2,)),
            dma((2,)),
            dma((2,)),
            dma((2,)),
        ],
        compiler_params=pltpu.CompilerParams(
            collective_id=0, has_side_effects=True, vmem_limit_bytes=56 * 2**20
        ),
    )(harmonic_offsets, right_side, coupling, eigen_basis, eigen_inverse, eigen_size.reshape(1, NC))
    return pl.pallas_call(
        combine,
        out_shape=jax.ShapeDtypeStruct((M, ROWS, KZ * R), full),
        in_specs=[vmem, anywhere],
        out_specs=anywhere,
        scratch_shapes=[
            pltpu.VMEM((M, ROWS, KZ * R), low),
            pltpu.VMEM((M, ROWS, KZ * R), low),
            pltpu.VMEM((M, ROWS, KZ * R), full),
            dma((2, M)),
            dma((M,)),
        ],
    )(steps, back)


def solution(mesh):
    in_specs = (P("sx", "sz", None), P("sx", None, None, None), P(), P(), P(), P())
    out_specs = P("sx", "sz", None)
    return jax.shard_map(shards, mesh=mesh, in_specs=in_specs, out_specs=out_specs, check_vma=False)
```

```python
import jax
import jax.numpy as jnp
from jax import lax
from jax.experimental import pallas as pl
from jax.experimental.pallas import tpu as pltpu
from jax.sharding import PartitionSpec as P

KX = 72
KZ = 128
NC = 256
H = 5
OFF = 6
R = 32
NX = 8
NZ = 16
M = KX // NX
ROWS = NC // NZ
COLS = KZ * R // NZ
SPANS = KZ // NZ
QUARTER = NC // 4
MESH = pl.DeviceIdType.MESH
WINDOW = 4
LATE = 0
LAG = 0
PACE = ((0, 2, 4, 4, 5), (8, 0, 4, 3, 0))


def device_at(x, y, z, core):
    return 2 * y + z % 2, 4 * x + 2 * (z // 2) + core


def wave_row(block, mode, group):
    index = block * M + mode
    signed_x = jnp.where(index < KX // 2, index, index - KX).astype(jnp.float32) * (4.0 / KX)
    column = lax.broadcasted_iota(jnp.int32, (1, COLS), 1)
    span = group * SPANS + column // R
    signed_z = jnp.where(span < KZ // 2, span, span - KZ).astype(jnp.float32) * (4.0 / KZ)
    return 1.0 + signed_x * signed_x + signed_z * signed_z


def kernel(
    offsets, right, coupling, basis, inverse, sizes, back, steps,
    start, factor, image, residual, blocks,
    search, sums, parts, row_sums, row_total, all_sums,
    load_sem, in_send, in_near, in_recv, out_send, out_near, out_recv, halo_send, halo_recv,
    block_send, block_recv, pass_send, row_send, row_recv, all_send, all_recv,
):
    sx, sz = lax.axis_index("sx"), lax.axis_index("sz")
    y, low_z = sx // 2, sx % 2
    x, core = sz // 4, sz % 2
    z = 2 * ((sz // 2) % 2) + low_z
    block = 2 * y + core
    group = 4 * x + z
    at_home = core == low_z
    away = core != low_z
    other = sz + 1 - 2 * core
    up = ((sx + 2 * core) % NX, other)
    down = ((sx + NX - 2 * (1 - core)) % NX, other)
    across = ((sx + NX + 4 * core - 2) % NX, other)

    load_blocks = pltpu.make_async_copy(coupling, blocks, load_sem.at[0])

    @pl.when(at_home)
    def _():
        load_blocks.start()

    barrier = pltpu.get_barrier_semaphore()

    place = NZ * low_z + sz

    @pl.loop(1, 2 * NZ)
    def _(k):
        to = (place + k) % (2 * NZ)
        pl.semaphore_signal(barrier, inc=1, device_id=(2 * y + to // NZ, to % NZ), device_id_type=MESH)

    @pl.loop(1, NX // 2)
    def _(k):
        pl.semaphore_signal(barrier, inc=1, device_id=((sx + 2 * k) % NX, sz), device_id_type=MESH)

    pl.semaphore_signal(barrier, inc=1, device_id=across, device_id_type=MESH)
    pl.semaphore_wait(barrier, 2 * NZ - 1 + NX // 2 - 1 + 1)

    def columns(index):
        return pl.ds(pl.multiple_of(index * COLS, COLS), COLS)

    def rows(index):
        return pl.ds(pl.multiple_of(index * ROWS, ROWS), ROWS)

    def quarter(index):
        return pl.ds(pl.multiple_of(index * QUARTER, QUARTER), QUARTER)

    def push(m, side):
        index = 2 * (x % 2) + side
        return pltpu.make_async_remote_copy(
            src_ref=coupling.at[m, :, quarter(index), :],
            dst_ref=blocks.at[m, :, quarter(index), :],
            send_sem=block_send.at[m, side],
            recv_sem=block_recv.at[m, index],
            device_id=device_at(x, y, (z + 1 + 2 * side) % 4, core),
            device_id_type=MESH,
        )

    def forward(m, side):
        index = 2 * (x % 2) + side
        return pltpu.make_async_remote_copy(
            src_ref=blocks.at[m, :, quarter(index), :],
            dst_ref=blocks.at[m, :, quarter(index), :],
            send_sem=pass_send.at[m, side],
            recv_sem=block_recv.at[m, index],
            device_id=(sx, (sz + 4 + 8 * side) % NZ),
            device_id_type=MESH,
        )

    def arrived(m, index):
        part = blocks.at[m, :, quarter(index), :]
        return pltpu.make_async_copy(part, part, block_recv.at[m, index])

    def pass_on(m):
        @pl.when(away)
        def _():
            for side in range(2):
                arrived(m, 2 * (x % 2) + side).wait()
                forward(m, side).start()

    def inward(m, k, send_sem):
        to = (group + k) % NZ
        return pltpu.make_async_remote_copy(
            src_ref=right.at[m, :, columns(to)],
            dst_ref=start.at[m, rows(sz), :],
            send_sem=send_sem,
            recv_sem=in_recv.at[m],
            device_id=device_at(to // 4, y, to % 4, low_z),
            device_id_type=MESH,
        )

    def send_mode(turn):
        m = (turn + 3 * low_z) % M

        @pl.when(at_home)
        def _():
            pltpu.make_async_copy(right.at[m, :, columns(group)], start.at[m, rows(sz), :], in_recv.at[m]).start()

        @pl.when(away)
        def _():
            inward(m, 0, in_near.at[m]).start()

        @pl.loop(1, NZ)
        def _(k):
            inward(m, k, in_send.at[m]).start()

        @pl.when(at_home & (turn >= LATE))
        def _():
            for side in range(2):
                push(turn - LATE, side).start()

    def outward(step, k, send_sem):
        to = (sz + k) % NZ
        return pltpu.make_async_remote_copy(
            src_ref=search.at[step, pl.ds(OFF, M), rows(to), :],
            dst_ref=back.at[step, :, :, columns(group)],
            send_sem=send_sem,
            recv_sem=out_recv.at[step],
            device_id=(block, to),
            device_id_type=MESH,
        )

    def send_near(step):
        @pl.when(at_home)
        def _():
            pltpu.make_async_copy(
                search.at[step, pl.ds(OFF, M), rows(sz), :], back.at[step, :, :, columns(group)], out_recv.at[step]
            ).start()

        @pl.when(away)
        def _():
            outward(step, 0, out_near.at[step]).start()

    def send_share(step, stage):
        begin = 1 + sum(PACE[step][:stage])

        @pl.loop(begin, begin + PACE[step][stage])
        def _(k):
            outward(step, k, out_send.at[step]).start()

    def send_one(step, stage, m):
        begin = 1 + sum(PACE[step][:stage])

        @pl.when(m < PACE[step][stage])
        def _():
            outward(step, begin + m, out_send.at[step]).start()

    def halo_down(step, m):
        return pltpu.make_async_remote_copy(
            src_ref=search.at[step, OFF + m],
            dst_ref=search.at[step, OFF + M + m],
            send_sem=halo_send.at[step, m],
            recv_sem=halo_recv.at[step, m],
            device_id=down,
            device_id_type=MESH,
        )

    def halo_up(step, m):
        return pltpu.make_async_remote_copy(
            src_ref=search.at[step, OFF + m],
            dst_ref=search.at[step, m - (M - OFF)],
            send_sem=halo_send.at[step, m + M - OFF],
            recv_sem=halo_recv.at[step, m + M - OFF],
            device_id=up,
            device_id_type=MESH,
        )

    def send_halo(step, m):
        @pl.when(m < OFF)
        def _():
            halo_down(step, m).start()

        @pl.when(m >= M - OFF)
        def _():
            halo_up(step, m).start()

    for m in range(WINDOW):
        send_mode(m)

    sizes_down = jnp.transpose(jnp.broadcast_to(sizes[...], (NC, NC)))

    @pl.loop(0, M)
    def _(m):
        factor[m] = -1.0 / (sizes_down + wave_row(block, m, group))

    def precondition(step, m, rounded):
        spectral = jnp.dot(inverse[...], rounded, preferred_element_type=jnp.float32)
        scaled = (spectral * factor[m]).astype(jnp.bfloat16)
        result = jnp.dot(basis[...], scaled, preferred_element_type=jnp.float32)
        search[step, OFF + m] = result.astype(jnp.bfloat16)

    def apply(step):
        @pl.loop(0, OFF)
        def _(m):
            halo_down(step, m).wait_recv()
            halo_up(step, m + M - OFF).wait_recv()

        sums[...] = jnp.zeros_like(sums)

        def one(m):
            total = -wave_row(block, m, group) * search[step, OFF + m].astype(jnp.float32)
            for h in range(H):
                total = total + jnp.dot(
                    blocks[m, h], search[step, OFF + m + offsets[h]], preferred_element_type=jnp.float32
                )
            if step == 0:
                image[m] = total
                before = start[m]
            else:
                before = residual[m]
            sums[0] += jnp.sum((total * before).reshape(NC // 8, 8, COLS), axis=0)
            sums[1] += jnp.sum((total * total).reshape(NC // 8, 8, COLS), axis=0)

        @pl.loop(0, M // 3)
        def _(turn):
            modes = [3 * turn + each for each in range(3)]
            if step == 0:

                @pl.when(away)
                def _():
                    for m in modes:
                        for side in range(2):
                            arrived(m, 2 * (1 - x % 2) + side).wait()

            for m in modes:
                send_one(step, 1, m)
            for m in modes:
                one(m)

    def row_copy(step, k):
        to = (place + k) % (2 * NZ)
        return pltpu.make_async_remote_copy(
            src_ref=parts.at[step],
            dst_ref=row_sums.at[step, place],
            send_sem=row_send.at[step],
            recv_sem=row_recv.at[step],
            device_id=(2 * y + to // NZ, to % NZ),
            device_id_type=MESH,
        )

    def all_copy(step, k):
        to = (y + k) % (NX // 2)
        return pltpu.make_async_remote_copy(
            src_ref=row_total.at[step],
            dst_ref=all_sums.at[step, y],
            send_sem=all_send.at[step],
            recv_sem=all_recv.at[step],
            device_id=(2 * to + low_z, sz),
            device_id_type=MESH,
        )

    first_half = lax.broadcasted_iota(jnp.int32, (8, 128), 1) < 64

    def step_size(step):
        def fold(value):
            value = value[:, :128] + value[:, 128:]
            value = value + pltpu.roll(value, 64, 1)
            return value + pltpu.roll(value, 32, 1)

        both = jnp.where(first_half, fold(sums[0]), fold(sums[1]))
        mine = jnp.sum(both, axis=0, keepdims=True)
        parts[step] = mine
        row_sums[step, place] = mine

        @pl.loop(1, 2 * NZ)
        def _(k):
            row_copy(step, k).start()

        send_share(step, 2)

        others = row_sums.at[step, pl.ds(0, 2 * NZ - 1)]
        pltpu.make_async_copy(others, others, row_recv.at[step]).wait()

        of_row = jnp.sum(row_sums[step], axis=0)
        row_total[step] = of_row
        all_sums[step, y] = of_row

        @pl.loop(1, NX // 2)
        def _(k):
            all_copy(step, k).start()

        send_share(step, 3)

        others = all_sums.at[step, pl.ds(0, NX // 2 - 1)]
        pltpu.make_async_copy(others, others, all_recv.at[step]).wait()

        of_all = all_sums[step, 0]
        for index in range(1, NX // 2):
            of_all = of_all + all_sums[step, index]
        of_all = jnp.broadcast_to(of_all, (8, 128))
        swapped = pltpu.roll(of_all, 64, 1)
        aligned = jnp.where(first_half, of_all, swapped)
        energy = jnp.where(first_half, swapped, of_all)
        return (aligned / (energy + 1e-6))[0:1]

    def sent(step):
        others = row_sums.at[step, pl.ds(0, 2 * NZ - 1)]
        pltpu.make_async_copy(others, others, row_send.at[step]).wait()
        others = all_sums.at[step, pl.ds(0, NX // 2 - 1)]
        pltpu.make_async_copy(others, others, all_send.at[step]).wait()

        @pl.loop(0, OFF)
        def _(m):
            halo_down(step, m).wait_send()
            halo_up(step, m + M - OFF).wait_send()

    def first_modes(begin, end):
        @pl.loop(begin, end)
        def _(turn):
            m = (turn + 3 * core) % M
            pltpu.make_async_copy(start.at[m], start.at[m], in_recv.at[m]).wait()

            @pl.when(turn + WINDOW < M)
            def _():
                send_mode(turn + WINDOW)

            precondition(0, m, start[m].astype(jnp.bfloat16))
            send_halo(0, m)

            @pl.when(turn >= LAG)
            def _():
                pass_on(turn - LAG)

    first_modes(0, M)

    @pl.loop(M - LAG, M)
    def _(m):
        pass_on(m)

    send_near(0)
    send_share(0, 0)

    @pl.when(at_home)
    def _():
        load_blocks.wait()

    apply(0)
    first = step_size(0)
    first_wide = jnp.concatenate([first, first], axis=1)

    @pl.loop(0, M // 3)
    def _(turn):
        modes = [(3 * turn + 3 * core + each) % M for each in range(3)]
        rounded = []
        for m in modes:
            left = start[m] - first_wide * image[m]
            residual[m] = left
            rounded.append(left.astype(jnp.bfloat16))
        spectral = [jnp.dot(inverse[...], each, preferred_element_type=jnp.float32) for each in rounded]
        scaled = [(each * factor[m]).astype(jnp.bfloat16) for each, m in zip(spectral, modes)]
        for each, m in zip(scaled, modes):
            result = jnp.dot(basis[...], each, preferred_element_type=jnp.float32)
            search[1, OFF + m] = result.astype(jnp.bfloat16)
        for each, m in enumerate(modes):
            send_halo(1, m)
            send_one(0, 4, 3 * turn + each)

    send_near(1)
    send_share(1, 0)
    @pl.loop(0, M)
    def _(m):
        part = start.at[m, pl.ds(0, NC - ROWS), :]
        pltpu.make_async_copy(part, part, in_send.at[m]).wait()

    @pl.when(at_home)
    def _():
        @pl.loop(0, M)
        def _(m):
            for side in range(2):
                push(m, side).wait_send()

    @pl.when(away)
    def _():
        @pl.loop(0, M)
        def _(m):
            inward(m, 0, in_near.at[m]).wait_send()
            for side in range(2):
                forward(m, side).wait_send()

    sent(0)
    apply(1)
    second = step_size(1)

    for step in range(2):
        pltpu.make_async_copy(back.at[step], back.at[step], out_recv.at[step]).wait()

    steps[0:1, :] = first
    steps[1:2, :] = second

    sent(1)
    for step in range(2):
        part = search.at[step, pl.ds(OFF, M), pl.ds(0, NC - ROWS), :]
        pltpu.make_async_copy(part, part, out_send.at[step]).wait()

    @pl.when(away)
    def _():
        for step in range(2):
            outward(step, 0, out_near.at[step]).wait_send()

def combine(steps, back, out, first, second, total, in_sem, out_sem):
    def fetch(m, step, into):
        return pltpu.make_async_copy(back.at[step, m], into.at[m], in_sem.at[step, m])

    def store(m):
        return pltpu.make_async_copy(total.at[m], out.at[m], out_sem.at[m])

    @pl.loop(0, M)
    def _(m):
        fetch(m, 0, first).start()
        fetch(m, 1, second).start()

    wide = jnp.tile(steps[...], (1, KZ * R // 128))

    @pl.loop(0, M)
    def _(m):
        fetch(m, 0, first).wait()
        fetch(m, 1, second).wait()
        total[m] = wide[0:1] * first[m].astype(jnp.float32) + wide[1:2] * second[m].astype(jnp.float32)
        store(m).start()

    @pl.loop(0, M)
    def _(m):
        store(m).wait()


def shards(right_side, coupling, harmonic_offsets, eigen_basis, eigen_inverse, eigen_size):
    vmem = pl.BlockSpec(memory_space=pltpu.VMEM)
    anywhere = pl.BlockSpec(memory_space=pl.ANY)
    low, full = jnp.bfloat16, jnp.float32
    dma = pltpu.SemaphoreType.DMA
    back, steps = pl.pallas_call(
        kernel,
        out_shape=(jax.ShapeDtypeStruct((2, M, ROWS, KZ * R), low), jax.ShapeDtypeStruct((2, 128), full)),
        in_specs=[pl.BlockSpec(memory_space=pltpu.SMEM), anywhere, anywhere, vmem, vmem, vmem],
        out_specs=(anywhere, vmem),
        scratch_shapes=[
            pltpu.VMEM((M, NC, COLS), full),
            pltpu.VMEM((M, NC, COLS), full),
            pltpu.VMEM((M, NC, COLS), full),
            pltpu.VMEM((M, NC, COLS), full),
            pltpu.VMEM((M, H, NC, NC), low),
            pltpu.VMEM((2, M + 2 * OFF, NC, COLS), low),
            pltpu.VMEM((2, 8, COLS), full),
            pltpu.VMEM((2, 1, 128), full),
            pltpu.VMEM((2, 2 * NZ, 1, 128), full),
            pltpu.VMEM((2, 1, 128), full),
            pltpu.VMEM((2, NX // 2, 1, 128), full),
            dma((1,)),
            dma((M,)),
            dma((M,)),
            dma((M,)),
            dma((2,)),
            dma((2,)),
            dma((2,)),
            dma((2, 2 * OFF)),
            dma((2, 2 * OFF)),
            dma((M, 2)),
            dma((M, 4)),
            dma((M, 2)),
            dma((2,)),
            dma((2,)),
            dma((2,)),
            dma((2,)),
        ],
        compiler_params=pltpu.CompilerParams(
            collective_id=0, has_side_effects=True, vmem_limit_bytes=56 * 2**20
        ),
    )(harmonic_offsets, right_side, coupling, eigen_basis, eigen_inverse, eigen_size.reshape(1, NC))
    return pl.pallas_call(
        combine,
        out_shape=jax.ShapeDtypeStruct((M, ROWS, KZ * R), full),
        in_specs=[vmem, anywhere],
        out_specs=anywhere,
        scratch_shapes=[
            pltpu.VMEM((M, ROWS, KZ * R), low),
            pltpu.VMEM((M, ROWS, KZ * R), low),
            pltpu.VMEM((M, ROWS, KZ * R), full),
            dma((2, M)),
            dma((M,)),
        ],
    )(steps, back)


def solution(mesh):
    in_specs = (P("sx", "sz", None), P("sx", None, None, None), P(), P(), P(), P())
    out_specs = P("sx", "sz", None)
    return jax.shard_map(shards, mesh=mesh, in_specs=in_specs, out_specs=out_specs, check_vma=False)
```

```python
import jax
import jax.numpy as jnp
from jax import lax
from jax.experimental import pallas as pl
from jax.experimental.pallas import tpu as pltpu
from jax.sharding import PartitionSpec as P

KX = 72
KZ = 128
NC = 256
H = 5
OFF = 6
R = 32
NX = 8
NZ = 16
M = KX // NX
ROWS = NC // NZ
COLS = KZ * R // NZ
SPANS = KZ // NZ
QUARTER = NC // 4
MESH = pl.DeviceIdType.MESH
WINDOW = 4
DIRECT = 1
LATE = 0
LAG = 0
PACE = ((0, 2, 4, 4, 5), (8, 0, 4, 3, 0))


def device_at(x, y, z, core):
    return 2 * y + z % 2, 4 * x + 2 * (z // 2) + core


def wave_row(block, mode, group):
    index = block * M + mode
    signed_x = jnp.where(index < KX // 2, index, index - KX).astype(jnp.float32) * (4.0 / KX)
    column = lax.broadcasted_iota(jnp.int32, (1, COLS), 1)
    span = group * SPANS + column // R
    signed_z = jnp.where(span < KZ // 2, span, span - KZ).astype(jnp.float32) * (4.0 / KZ)
    return 1.0 + signed_x * signed_x + signed_z * signed_z


def kernel(
    offsets, right, coupling, basis, inverse, sizes, back, steps,
    start, factor, image, residual, blocks,
    search, sums, parts, row_sums, row_total, all_sums,
    load_sem, in_send, in_near, in_recv, out_send, out_near, out_recv, halo_send, halo_recv,
    block_send, whole_send, block_recv, pass_send, row_send, row_recv, all_send, all_recv,
):
    sx, sz = lax.axis_index("sx"), lax.axis_index("sz")
    y, low_z = sx // 2, sx % 2
    x, core = sz // 4, sz % 2
    z = 2 * ((sz // 2) % 2) + low_z
    block = 2 * y + core
    group = 4 * x + z
    at_home = core == low_z
    away = core != low_z
    other = sz + 1 - 2 * core
    up = ((sx + 2 * core) % NX, other)
    down = ((sx + NX - 2 * (1 - core)) % NX, other)
    across = ((sx + NX + 4 * core - 2) % NX, other)

    load_blocks = pltpu.make_async_copy(coupling, blocks, load_sem.at[0])

    @pl.when(at_home)
    def _():
        load_blocks.start()

    barrier = pltpu.get_barrier_semaphore()

    place = NZ * low_z + sz

    @pl.loop(1, 2 * NZ)
    def _(k):
        to = (place + k) % (2 * NZ)
        pl.semaphore_signal(barrier, inc=1, device_id=(2 * y + to // NZ, to % NZ), device_id_type=MESH)

    @pl.loop(1, NX // 2)
    def _(k):
        pl.semaphore_signal(barrier, inc=1, device_id=((sx + 2 * k) % NX, sz), device_id_type=MESH)

    pl.semaphore_signal(barrier, inc=1, device_id=across, device_id_type=MESH)
    pl.semaphore_wait(barrier, 2 * NZ - 1 + NX // 2 - 1 + 1)

    def columns(index):
        return pl.ds(pl.multiple_of(index * COLS, COLS), COLS)

    def rows(index):
        return pl.ds(pl.multiple_of(index * ROWS, ROWS), ROWS)

    def quarter(index):
        return pl.ds(pl.multiple_of(index * QUARTER, QUARTER), QUARTER)

    def push(m, side):
        index = 2 * (x % 2) + side
        return pltpu.make_async_remote_copy(
            src_ref=coupling.at[m, :, quarter(index), :],
            dst_ref=blocks.at[m, :, quarter(index), :],
            send_sem=block_send.at[m, side],
            recv_sem=block_recv.at[m, index],
            device_id=device_at(x, y, (z + 1 + 2 * side) % 4, core),
            device_id_type=MESH,
        )

    def push_whole(m, index):
        return pltpu.make_async_remote_copy(
            src_ref=coupling.at[m, :, quarter(index), :],
            dst_ref=blocks.at[m, :, quarter(index), :],
            send_sem=whole_send.at[m, index],
            recv_sem=block_recv.at[m, index],
            device_id=device_at(x, y, (z + 1 + 2 * (index // 2)) % 4, core),
            device_id_type=MESH,
        )

    def forward(m, side):
        index = 2 * (x % 2) + side
        return pltpu.make_async_remote_copy(
            src_ref=blocks.at[m, :, quarter(index), :],
            dst_ref=blocks.at[m, :, quarter(index), :],
            send_sem=pass_send.at[m, side],
            recv_sem=block_recv.at[m, index],
            device_id=(sx, (sz + 4 + 8 * side) % NZ),
            device_id_type=MESH,
        )

    def arrived(m, index):
        part = blocks.at[m, :, quarter(index), :]
        return pltpu.make_async_copy(part, part, block_recv.at[m, index])

    def pass_on(m):
        @pl.when(away & (m < M - DIRECT))
        def _():
            for side in range(2):
                arrived(m, 2 * (x % 2) + side).wait()
                forward(m, side).start()

    def inward(m, k, send_sem):
        to = (group + k) % NZ
        return pltpu.make_async_remote_copy(
            src_ref=right.at[m, :, columns(to)],
            dst_ref=start.at[m, rows(sz), :],
            send_sem=send_sem,
            recv_sem=in_recv.at[m],
            device_id=device_at(to // 4, y, to % 4, low_z),
            device_id_type=MESH,
        )

    def send_mode(turn):
        m = (turn + 3 * low_z) % M

        @pl.when(at_home)
        def _():
            pltpu.make_async_copy(right.at[m, :, columns(group)], start.at[m, rows(sz), :], in_recv.at[m]).start()

        @pl.when(away)
        def _():
            inward(m, 0, in_near.at[m]).start()

        @pl.loop(1, NZ)
        def _(k):
            inward(m, k, in_send.at[m]).start()

        @pl.when(at_home & (turn < M - DIRECT))
        def _():
            for side in range(2):
                push(turn, side).start()

        @pl.when(at_home & (turn >= M - DIRECT))
        def _():
            for index in range(4):
                push_whole(turn, index).start()

    def outward(step, k, send_sem):
        to = (sz + k) % NZ
        return pltpu.make_async_remote_copy(
            src_ref=search.at[step, pl.ds(OFF, M), rows(to), :],
            dst_ref=back.at[step, :, :, columns(group)],
            send_sem=send_sem,
            recv_sem=out_recv.at[step],
            device_id=(block, to),
            device_id_type=MESH,
        )

    def send_near(step):
        @pl.when(at_home)
        def _():
            pltpu.make_async_copy(
                search.at[step, pl.ds(OFF, M), rows(sz), :], back.at[step, :, :, columns(group)], out_recv.at[step]
            ).start()

        @pl.when(away)
        def _():
            outward(step, 0, out_near.at[step]).start()

    def send_share(step, stage):
        begin = 1 + sum(PACE[step][:stage])

        @pl.loop(begin, begin + PACE[step][stage])
        def _(k):
            outward(step, k, out_send.at[step]).start()

    def send_one(step, stage, m):
        begin = 1 + sum(PACE[step][:stage])

        @pl.when(m < PACE[step][stage])
        def _():
            outward(step, begin + m, out_send.at[step]).start()

    def halo_down(step, m):
        return pltpu.make_async_remote_copy(
            src_ref=search.at[step, OFF + m],
            dst_ref=search.at[step, OFF + M + m],
            send_sem=halo_send.at[step, m],
            recv_sem=halo_recv.at[step, m],
            device_id=down,
            device_id_type=MESH,
        )

    def halo_up(step, m):
        return pltpu.make_async_remote_copy(
            src_ref=search.at[step, OFF + m],
            dst_ref=search.at[step, m - (M - OFF)],
            send_sem=halo_send.at[step, m + M - OFF],
            recv_sem=halo_recv.at[step, m + M - OFF],
            device_id=up,
            device_id_type=MESH,
        )

    def send_halo(step, m):
        @pl.when(m < OFF)
        def _():
            halo_down(step, m).start()

        @pl.when(m >= M - OFF)
        def _():
            halo_up(step, m).start()

    for m in range(WINDOW):
        send_mode(m)

    sizes_down = jnp.transpose(jnp.broadcast_to(sizes[...], (NC, NC)))

    @pl.loop(0, M)
    def _(m):
        factor[m] = -1.0 / (sizes_down + wave_row(block, m, group))

    def precondition(step, m, rounded):
        spectral = jnp.dot(inverse[...], rounded, preferred_element_type=jnp.float32)
        scaled = (spectral * factor[m]).astype(jnp.bfloat16)
        result = jnp.dot(basis[...], scaled, preferred_element_type=jnp.float32)
        search[step, OFF + m] = result.astype(jnp.bfloat16)

    def apply(step):
        @pl.loop(0, OFF)
        def _(m):
            halo_down(step, m).wait_recv()
            halo_up(step, m + M - OFF).wait_recv()

        sums[...] = jnp.zeros_like(sums)

        def one(m):
            total = -wave_row(block, m, group) * search[step, OFF + m].astype(jnp.float32)
            for h in range(H):
                total = total + jnp.dot(
                    blocks[m, h], search[step, OFF + m + offsets[h]], preferred_element_type=jnp.float32
                )
            if step == 0:
                image[m] = total
                before = start[m]
            else:
                before = residual[m]
            sums[0] += jnp.sum((total * before).reshape(NC // 8, 8, COLS), axis=0)
            sums[1] += jnp.sum((total * total).reshape(NC // 8, 8, COLS), axis=0)

        @pl.loop(0, M // 3)
        def _(turn):
            modes = [3 * turn + each for each in range(3)]
            if step == 0:

                @pl.when(away)
                def _():
                    for m in modes:
                        for side in range(2):
                            arrived(m, 2 * (1 - x % 2) + side).wait()

                        @pl.when(m >= M - DIRECT)
                        def _():
                            for side in range(2):
                                arrived(m, 2 * (x % 2) + side).wait()

            for m in modes:
                send_one(step, 1, m)
            for m in modes:
                one(m)

    def row_copy(step, k):
        to = (place + k) % (2 * NZ)
        return pltpu.make_async_remote_copy(
            src_ref=parts.at[step],
            dst_ref=row_sums.at[step, place],
            send_sem=row_send.at[step],
            recv_sem=row_recv.at[step],
            device_id=(2 * y + to // NZ, to % NZ),
            device_id_type=MESH,
        )

    def all_copy(step, k):
        to = (y + k) % (NX // 2)
        return pltpu.make_async_remote_copy(
            src_ref=row_total.at[step],
            dst_ref=all_sums.at[step, y],
            send_sem=all_send.at[step],
            recv_sem=all_recv.at[step],
            device_id=(2 * to + low_z, sz),
            device_id_type=MESH,
        )

    first_half = lax.broadcasted_iota(jnp.int32, (8, 128), 1) < 64

    def step_size(step):
        def fold(value):
            value = value[:, :128] + value[:, 128:]
            value = value + pltpu.roll(value, 64, 1)
            return value + pltpu.roll(value, 32, 1)

        both = jnp.where(first_half, fold(sums[0]), fold(sums[1]))
        mine = jnp.sum(both, axis=0, keepdims=True)
        parts[step] = mine
        row_sums[step, place] = mine

        @pl.loop(1, 2 * NZ)
        def _(k):
            row_copy(step, k).start()

        send_share(step, 2)

        others = row_sums.at[step, pl.ds(0, 2 * NZ - 1)]
        pltpu.make_async_copy(others, others, row_recv.at[step]).wait()

        of_row = jnp.sum(row_sums[step], axis=0)
        row_total[step] = of_row
        all_sums[step, y] = of_row

        @pl.loop(1, NX // 2)
        def _(k):
            all_copy(step, k).start()

        send_share(step, 3)

        others = all_sums.at[step, pl.ds(0, NX // 2 - 1)]
        pltpu.make_async_copy(others, others, all_recv.at[step]).wait()

        of_all = all_sums[step, 0]
        for index in range(1, NX // 2):
            of_all = of_all + all_sums[step, index]
        of_all = jnp.broadcast_to(of_all, (8, 128))
        swapped = pltpu.roll(of_all, 64, 1)
        aligned = jnp.where(first_half, of_all, swapped)
        energy = jnp.where(first_half, swapped, of_all)
        return (aligned / (energy + 1e-6))[0:1]

    def sent(step):
        others = row_sums.at[step, pl.ds(0, 2 * NZ - 1)]
        pltpu.make_async_copy(others, others, row_send.at[step]).wait()
        others = all_sums.at[step, pl.ds(0, NX // 2 - 1)]
        pltpu.make_async_copy(others, others, all_send.at[step]).wait()

        @pl.loop(0, OFF)
        def _(m):
            halo_down(step, m).wait_send()
            halo_up(step, m + M - OFF).wait_send()

    def first_modes(begin, end):
        @pl.loop(begin, end)
        def _(turn):
            m = (turn + 3 * core) % M
            pltpu.make_async_copy(start.at[m], start.at[m], in_recv.at[m]).wait()

            @pl.when(turn + WINDOW < M)
            def _():
                send_mode(turn + WINDOW)

            precondition(0, m, start[m].astype(jnp.bfloat16))
            send_halo(0, m)

            @pl.when(turn >= LAG)
            def _():
                pass_on(turn - LAG)

    first_modes(0, M)

    @pl.loop(M - LAG, M)
    def _(m):
        pass_on(m)

    send_near(0)
    send_share(0, 0)

    @pl.when(at_home)
    def _():
        load_blocks.wait()

    apply(0)
    first = step_size(0)
    first_wide = jnp.concatenate([first, first], axis=1)

    @pl.loop(0, M // 3)
    def _(turn):
        modes = [(3 * turn + 3 * core + each) % M for each in range(3)]
        rounded = []
        for m in modes:
            left = start[m] - first_wide * image[m]
            residual[m] = left
            rounded.append(left.astype(jnp.bfloat16))
        spectral = [jnp.dot(inverse[...], each, preferred_element_type=jnp.float32) for each in rounded]
        scaled = [(each * factor[m]).astype(jnp.bfloat16) for each, m in zip(spectral, modes)]
        for each, m in zip(scaled, modes):
            result = jnp.dot(basis[...], each, preferred_element_type=jnp.float32)
            search[1, OFF + m] = result.astype(jnp.bfloat16)
        for each, m in enumerate(modes):
            send_halo(1, m)
            send_one(0, 4, 3 * turn + each)

    send_near(1)
    send_share(1, 0)
    @pl.loop(0, M)
    def _(m):
        part = start.at[m, pl.ds(0, NC - ROWS), :]
        pltpu.make_async_copy(part, part, in_send.at[m]).wait()

    @pl.when(at_home)
    def _():
        @pl.loop(0, M - DIRECT)
        def _(m):
            for side in range(2):
                push(m, side).wait_send()

        @pl.loop(M - DIRECT, M)
        def _(m):
            for index in range(4):
                push_whole(m, index).wait_send()

    @pl.when(away)
    def _():
        @pl.loop(0, M)
        def _(m):
            inward(m, 0, in_near.at[m]).wait_send()

        @pl.loop(0, M - DIRECT)
        def _(m):
            for side in range(2):
                forward(m, side).wait_send()

    sent(0)
    apply(1)
    second = step_size(1)

    for step in range(2):
        pltpu.make_async_copy(back.at[step], back.at[step], out_recv.at[step]).wait()

    steps[0:1, :] = first
    steps[1:2, :] = second

    sent(1)
    for step in range(2):
        part = search.at[step, pl.ds(OFF, M), pl.ds(0, NC - ROWS), :]
        pltpu.make_async_copy(part, part, out_send.at[step]).wait()

    @pl.when(away)
    def _():
        for step in range(2):
            outward(step, 0, out_near.at[step]).wait_send()

def combine(steps, back, out, first, second, total, in_sem, out_sem):
    def fetch(m, step, into):
        return pltpu.make_async_copy(back.at[step, m], into.at[m], in_sem.at[step, m])

    def store(m):
        return pltpu.make_async_copy(total.at[m], out.at[m], out_sem.at[m])

    @pl.loop(0, M)
    def _(m):
        fetch(m, 0, first).start()
        fetch(m, 1, second).start()

    wide = jnp.tile(steps[...], (1, KZ * R // 128))

    @pl.loop(0, M)
    def _(m):
        fetch(m, 0, first).wait()
        fetch(m, 1, second).wait()
        total[m] = wide[0:1] * first[m].astype(jnp.float32) + wide[1:2] * second[m].astype(jnp.float32)
        store(m).start()

    @pl.loop(0, M)
    def _(m):
        store(m).wait()


def shards(right_side, coupling, harmonic_offsets, eigen_basis, eigen_inverse, eigen_size):
    vmem = pl.BlockSpec(memory_space=pltpu.VMEM)
    anywhere = pl.BlockSpec(memory_space=pl.ANY)
    low, full = jnp.bfloat16, jnp.float32
    dma = pltpu.SemaphoreType.DMA
    back, steps = pl.pallas_call(
        kernel,
        out_shape=(jax.ShapeDtypeStruct((2, M, ROWS, KZ * R), low), jax.ShapeDtypeStruct((2, 128), full)),
        in_specs=[pl.BlockSpec(memory_space=pltpu.SMEM), anywhere, anywhere, vmem, vmem, vmem],
        out_specs=(anywhere, vmem),
        scratch_shapes=[
            pltpu.VMEM((M, NC, COLS), full),
            pltpu.VMEM((M, NC, COLS), full),
            pltpu.VMEM((M, NC, COLS), full),
            pltpu.VMEM((M, NC, COLS), full),
            pltpu.VMEM((M, H, NC, NC), low),
            pltpu.VMEM((2, M + 2 * OFF, NC, COLS), low),
            pltpu.VMEM((2, 8, COLS), full),
            pltpu.VMEM((2, 1, 128), full),
            pltpu.VMEM((2, 2 * NZ, 1, 128), full),
            pltpu.VMEM((2, 1, 128), full),
            pltpu.VMEM((2, NX // 2, 1, 128), full),
            dma((1,)),
            dma((M,)),
            dma((M,)),
            dma((M,)),
            dma((2,)),
            dma((2,)),
            dma((2,)),
            dma((2, 2 * OFF)),
            dma((2, 2 * OFF)),
            dma((M, 2)),
            dma((M, 4)),
            dma((M, 4)),
            dma((M, 2)),
            dma((2,)),
            dma((2,)),
            dma((2,)),
            dma((2,)),
        ],
        compiler_params=pltpu.CompilerParams(
            collective_id=0, has_side_effects=True, vmem_limit_bytes=56 * 2**20
        ),
    )(harmonic_offsets, right_side, coupling, eigen_basis, eigen_inverse, eigen_size.reshape(1, NC))
    return pl.pallas_call(
        combine,
        out_shape=jax.ShapeDtypeStruct((M, ROWS, KZ * R), full),
        in_specs=[vmem, anywhere],
        out_specs=anywhere,
        scratch_shapes=[
            pltpu.VMEM((M, ROWS, KZ * R), low),
            pltpu.VMEM((M, ROWS, KZ * R), low),
            pltpu.VMEM((M, ROWS, KZ * R), full),
            dma((2, M)),
            dma((M,)),
        ],
    )(steps, back)


def solution(mesh):
    in_specs = (P("sx", "sz", None), P("sx", None, None, None), P(), P(), P(), P())
    out_specs = P("sx", "sz", None)
    return jax.shard_map(shards, mesh=mesh, in_specs=in_specs, out_specs=out_specs, check_vma=False)
```

```python
import jax
import jax.numpy as jnp
from jax import lax
from jax.experimental import pallas as pl
from jax.experimental.pallas import tpu as pltpu
from jax.sharding import PartitionSpec as P

KX = 72
KZ = 128
NC = 256
H = 5
OFF = 6
R = 32
NX = 8
NZ = 16
M = KX // NX
ROWS = NC // NZ
COLS = KZ * R // NZ
SPANS = KZ // NZ
QUARTER = NC // 4
MESH = pl.DeviceIdType.MESH
WINDOW = 4
DIRECT = 1
LATE = 0
LAG = 0
PACE = ((0, 2, 4, 4, 5), (8, 0, 4, 3, 0))


def device_at(x, y, z, core):
    return 2 * y + z % 2, 4 * x + 2 * (z // 2) + core


def wave_row(block, mode, group):
    index = block * M + mode
    signed_x = jnp.where(index < KX // 2, index, index - KX).astype(jnp.float32) * (4.0 / KX)
    column = lax.broadcasted_iota(jnp.int32, (1, COLS), 1)
    span = group * SPANS + column // R
    signed_z = jnp.where(span < KZ // 2, span, span - KZ).astype(jnp.float32) * (4.0 / KZ)
    return 1.0 + signed_x * signed_x + signed_z * signed_z


def kernel(
    offsets, right, coupling, basis, inverse, sizes, back, steps,
    start, factor, image, residual, blocks,
    search, sums, parts, row_sums, row_total, all_sums,
    load_sem, in_send, in_near, in_recv, out_send, out_near, out_recv, halo_send, halo_recv,
    block_send, whole_send, block_recv, pass_send, row_send, row_recv, all_send, all_recv,
):
    sx, sz = lax.axis_index("sx"), lax.axis_index("sz")
    y, low_z = sx // 2, sx % 2
    x, core = sz // 4, sz % 2
    z = 2 * ((sz // 2) % 2) + low_z
    block = 2 * y + core
    group = 4 * x + z
    at_home = core == low_z
    away = core != low_z
    other = sz + 1 - 2 * core
    up = ((sx + 2 * core) % NX, other)
    down = ((sx + NX - 2 * (1 - core)) % NX, other)
    across = ((sx + NX + 4 * core - 2) % NX, other)

    load_blocks = pltpu.make_async_copy(coupling, blocks, load_sem.at[0])

    @pl.when(at_home)
    def _():
        load_blocks.start()

    barrier = pltpu.get_barrier_semaphore()

    place = NZ * low_z + sz

    @pl.loop(1, 2 * NZ)
    def _(k):
        to = (place + k) % (2 * NZ)
        pl.semaphore_signal(barrier, inc=1, device_id=(2 * y + to // NZ, to % NZ), device_id_type=MESH)

    @pl.loop(1, NX // 2)
    def _(k):
        pl.semaphore_signal(barrier, inc=1, device_id=((sx + 2 * k) % NX, sz), device_id_type=MESH)

    pl.semaphore_signal(barrier, inc=1, device_id=across, device_id_type=MESH)
    pl.semaphore_wait(barrier, 2 * NZ - 1 + NX // 2 - 1 + 1)

    def columns(index):
        return pl.ds(pl.multiple_of(index * COLS, COLS), COLS)

    def rows(index):
        return pl.ds(pl.multiple_of(index * ROWS, ROWS), ROWS)

    def quarter(index):
        return pl.ds(pl.multiple_of(index * QUARTER, QUARTER), QUARTER)

    def push(m, side):
        index = 2 * (x % 2) + side
        return pltpu.make_async_remote_copy(
            src_ref=coupling.at[m, :, quarter(index), :],
            dst_ref=blocks.at[m, :, quarter(index), :],
            send_sem=block_send.at[m, side],
            recv_sem=block_recv.at[m, index],
            device_id=device_at(x, y, (z + 1 + 2 * side) % 4, core),
            device_id_type=MESH,
        )

    def push_whole(m, index):
        return pltpu.make_async_remote_copy(
            src_ref=coupling.at[m, :, quarter(index), :],
            dst_ref=blocks.at[m, :, quarter(index), :],
            send_sem=whole_send.at[m, index],
            recv_sem=block_recv.at[m, index],
            device_id=device_at(x, y, (z + 1 + 2 * (index // 2)) % 4, core),
            device_id_type=MESH,
        )

    def forward(m, side):
        index = 2 * (x % 2) + side
        return pltpu.make_async_remote_copy(
            src_ref=blocks.at[m, :, quarter(index), :],
            dst_ref=blocks.at[m, :, quarter(index), :],
            send_sem=pass_send.at[m, side],
            recv_sem=block_recv.at[m, index],
            device_id=(sx, (sz + 4 + 8 * side) % NZ),
            device_id_type=MESH,
        )

    def arrived(m, index):
        part = blocks.at[m, :, quarter(index), :]
        return pltpu.make_async_copy(part, part, block_recv.at[m, index])

    def pass_on(m):
        @pl.when(away & (m < M - DIRECT))
        def _():
            for side in range(2):
                arrived(m, 2 * (x % 2) + side).wait()
                forward(m, side).start()

    def inward(m, k, send_sem):
        to = (group + (1 - core) * k + core * (NZ - k)) % NZ
        return pltpu.make_async_remote_copy(
            src_ref=right.at[m, :, columns(to)],
            dst_ref=start.at[m, rows(sz), :],
            send_sem=send_sem,
            recv_sem=in_recv.at[m],
            device_id=device_at(to // 4, y, to % 4, low_z),
            device_id_type=MESH,
        )

    def send_mode(turn):
        m = (turn + 3 * low_z) % M

        @pl.when(at_home)
        def _():
            pltpu.make_async_copy(right.at[m, :, columns(group)], start.at[m, rows(sz), :], in_recv.at[m]).start()

        @pl.when(away)
        def _():
            inward(m, 0, in_near.at[m]).start()

        @pl.loop(1, NZ)
        def _(k):
            inward(m, k, in_send.at[m]).start()

        @pl.when(at_home & (turn < M - DIRECT))
        def _():
            for side in range(2):
                push(turn, side).start()

        @pl.when(at_home & (turn >= M - DIRECT))
        def _():
            for index in range(4):
                push_whole(turn, index).start()

    def outward(step, k, send_sem):
        to = (sz + k) % NZ
        return pltpu.make_async_remote_copy(
            src_ref=search.at[step, pl.ds(OFF, M), rows(to), :],
            dst_ref=back.at[step, :, :, columns(group)],
            send_sem=send_sem,
            recv_sem=out_recv.at[step],
            device_id=(block, to),
            device_id_type=MESH,
        )

    def send_near(step):
        @pl.when(at_home)
        def _():
            pltpu.make_async_copy(
                search.at[step, pl.ds(OFF, M), rows(sz), :], back.at[step, :, :, columns(group)], out_recv.at[step]
            ).start()

        @pl.when(away)
        def _():
            outward(step, 0, out_near.at[step]).start()

    def send_share(step, stage):
        begin = 1 + sum(PACE[step][:stage])

        @pl.loop(begin, begin + PACE[step][stage])
        def _(k):
            outward(step, k, out_send.at[step]).start()

    def send_one(step, stage, m):
        begin = 1 + sum(PACE[step][:stage])

        @pl.when(m < PACE[step][stage])
        def _():
            outward(step, begin + m, out_send.at[step]).start()

    def halo_down(step, m):
        return pltpu.make_async_remote_copy(
            src_ref=search.at[step, OFF + m],
            dst_ref=search.at[step, OFF + M + m],
            send_sem=halo_send.at[step, m],
            recv_sem=halo_recv.at[step, m],
            device_id=down,
            device_id_type=MESH,
        )

    def halo_up(step, m):
        return pltpu.make_async_remote_copy(
            src_ref=search.at[step, OFF + m],
            dst_ref=search.at[step, m - (M - OFF)],
            send_sem=halo_send.at[step, m + M - OFF],
            recv_sem=halo_recv.at[step, m + M - OFF],
            device_id=up,
            device_id_type=MESH,
        )

    def send_halo(step, m):
        @pl.when(m < OFF)
        def _():
            halo_down(step, m).start()

        @pl.when(m >= M - OFF)
        def _():
            halo_up(step, m).start()

    for m in range(WINDOW):
        send_mode(m)

    sizes_down = jnp.transpose(jnp.broadcast_to(sizes[...], (NC, NC)))

    @pl.loop(0, M)
    def _(m):
        factor[m] = -1.0 / (sizes_down + wave_row(block, m, group))

    def precondition(step, m, rounded):
        spectral = jnp.dot(inverse[...], rounded, preferred_element_type=jnp.float32)
        scaled = (spectral * factor[m]).astype(jnp.bfloat16)
        result = jnp.dot(basis[...], scaled, preferred_element_type=jnp.float32)
        search[step, OFF + m] = result.astype(jnp.bfloat16)

    def apply(step):
        @pl.loop(0, OFF)
        def _(m):
            halo_down(step, m).wait_recv()
            halo_up(step, m + M - OFF).wait_recv()

        sums[...] = jnp.zeros_like(sums)

        def one(m):
            total = -wave_row(block, m, group) * search[step, OFF + m].astype(jnp.float32)
            for h in range(H):
                total = total + jnp.dot(
                    blocks[m, h], search[step, OFF + m + offsets[h]], preferred_element_type=jnp.float32
                )
            if step == 0:
                image[m] = total
                before = start[m]
            else:
                before = residual[m]
            sums[0] += jnp.sum((total * before).reshape(NC // 8, 8, COLS), axis=0)
            sums[1] += jnp.sum((total * total).reshape(NC // 8, 8, COLS), axis=0)

        @pl.loop(0, M // 3)
        def _(turn):
            modes = [3 * turn + each for each in range(3)]
            if step == 0:

                @pl.when(away)
                def _():
                    for m in modes:
                        for side in range(2):
                            arrived(m, 2 * (1 - x % 2) + side).wait()

                        @pl.when(m >= M - DIRECT)
                        def _():
                            for side in range(2):
                                arrived(m, 2 * (x % 2) + side).wait()

            for m in modes:
                send_one(step, 1, m)
            for m in modes:
                one(m)

    def row_copy(step, k):
        to = (place + k) % (2 * NZ)
        return pltpu.make_async_remote_copy(
            src_ref=parts.at[step],
            dst_ref=row_sums.at[step, place],
            send_sem=row_send.at[step],
            recv_sem=row_recv.at[step],
            device_id=(2 * y + to // NZ, to % NZ),
            device_id_type=MESH,
        )

    def all_copy(step, k):
        to = (y + k) % (NX // 2)
        return pltpu.make_async_remote_copy(
            src_ref=row_total.at[step],
            dst_ref=all_sums.at[step, y],
            send_sem=all_send.at[step],
            recv_sem=all_recv.at[step],
            device_id=(2 * to + low_z, sz),
            device_id_type=MESH,
        )

    first_half = lax.broadcasted_iota(jnp.int32, (8, 128), 1) < 64

    def step_size(step):
        def fold(value):
            value = value[:, :128] + value[:, 128:]
            value = value + pltpu.roll(value, 64, 1)
            return value + pltpu.roll(value, 32, 1)

        both = jnp.where(first_half, fold(sums[0]), fold(sums[1]))
        mine = jnp.sum(both, axis=0, keepdims=True)
        parts[step] = mine
        row_sums[step, place] = mine

        @pl.loop(1, 2 * NZ)
        def _(k):
            row_copy(step, k).start()

        send_share(step, 2)

        others = row_sums.at[step, pl.ds(0, 2 * NZ - 1)]
        pltpu.make_async_copy(others, others, row_recv.at[step]).wait()

        of_row = jnp.sum(row_sums[step], axis=0)
        row_total[step] = of_row
        all_sums[step, y] = of_row

        @pl.loop(1, NX // 2)
        def _(k):
            all_copy(step, k).start()

        send_share(step, 3)

        others = all_sums.at[step, pl.ds(0, NX // 2 - 1)]
        pltpu.make_async_copy(others, others, all_recv.at[step]).wait()

        of_all = all_sums[step, 0]
        for index in range(1, NX // 2):
            of_all = of_all + all_sums[step, index]
        of_all = jnp.broadcast_to(of_all, (8, 128))
        swapped = pltpu.roll(of_all, 64, 1)
        aligned = jnp.where(first_half, of_all, swapped)
        energy = jnp.where(first_half, swapped, of_all)
        return (aligned / (energy + 1e-6))[0:1]

    def sent(step):
        others = row_sums.at[step, pl.ds(0, 2 * NZ - 1)]
        pltpu.make_async_copy(others, others, row_send.at[step]).wait()
        others = all_sums.at[step, pl.ds(0, NX // 2 - 1)]
        pltpu.make_async_copy(others, others, all_send.at[step]).wait()

        @pl.loop(0, OFF)
        def _(m):
            halo_down(step, m).wait_send()
            halo_up(step, m + M - OFF).wait_send()

    def first_modes(begin, end):
        @pl.loop(begin, end)
        def _(turn):
            m = (turn + 3 * core) % M
            pltpu.make_async_copy(start.at[m], start.at[m], in_recv.at[m]).wait()

            @pl.when(turn + WINDOW < M)
            def _():
                send_mode(turn + WINDOW)

            precondition(0, m, start[m].astype(jnp.bfloat16))
            send_halo(0, m)

            @pl.when(turn >= LAG)
            def _():
                pass_on(turn - LAG)

    first_modes(0, M)

    @pl.loop(M - LAG, M)
    def _(m):
        pass_on(m)

    send_near(0)
    send_share(0, 0)

    @pl.when(at_home)
    def _():
        load_blocks.wait()

    apply(0)
    first = step_size(0)
    first_wide = jnp.concatenate([first, first], axis=1)

    @pl.loop(0, M // 3)
    def _(turn):
        modes = [(3 * turn + 3 * core + each) % M for each in range(3)]
        rounded = []
        for m in modes:
            left = start[m] - first_wide * image[m]
            residual[m] = left
            rounded.append(left.astype(jnp.bfloat16))
        spectral = [jnp.dot(inverse[...], each, preferred_element_type=jnp.float32) for each in rounded]
        scaled = [(each * factor[m]).astype(jnp.bfloat16) for each, m in zip(spectral, modes)]
        for each, m in zip(scaled, modes):
            result = jnp.dot(basis[...], each, preferred_element_type=jnp.float32)
            search[1, OFF + m] = result.astype(jnp.bfloat16)
            send_halo(1, m)
        for each in range(3):
            send_one(0, 4, 3 * turn + each)

    send_near(1)
    send_share(1, 0)
    @pl.loop(0, M)
    def _(m):
        part = start.at[m, pl.ds(0, NC - ROWS), :]
        pltpu.make_async_copy(part, part, in_send.at[m]).wait()

    @pl.when(at_home)
    def _():
        @pl.loop(0, M - DIRECT)
        def _(m):
            for side in range(2):
                push(m, side).wait_send()

        @pl.loop(M - DIRECT, M)
        def _(m):
            for index in range(4):
                push_whole(m, index).wait_send()

    @pl.when(away)
    def _():
        @pl.loop(0, M)
        def _(m):
            inward(m, 0, in_near.at[m]).wait_send()

        @pl.loop(0, M - DIRECT)
        def _(m):
            for side in range(2):
                forward(m, side).wait_send()

    sent(0)
    apply(1)
    second = step_size(1)

    for step in range(2):
        pltpu.make_async_copy(back.at[step], back.at[step], out_recv.at[step]).wait()

    steps[0:1, :] = first
    steps[1:2, :] = second

    sent(1)
    for step in range(2):
        part = search.at[step, pl.ds(OFF, M), pl.ds(0, NC - ROWS), :]
        pltpu.make_async_copy(part, part, out_send.at[step]).wait()

    @pl.when(away)
    def _():
        for step in range(2):
            outward(step, 0, out_near.at[step]).wait_send()

def combine(steps, back, out, first, second, total, in_sem, out_sem):
    def fetch(m, step, into):
        return pltpu.make_async_copy(back.at[step, m], into.at[m], in_sem.at[step, m])

    def store(m):
        return pltpu.make_async_copy(total.at[m], out.at[m], out_sem.at[m])

    @pl.loop(0, M)
    def _(m):
        fetch(m, 0, first).start()
        fetch(m, 1, second).start()

    wide = jnp.tile(steps[...], (1, KZ * R // 128))

    @pl.loop(0, M)
    def _(m):
        fetch(m, 0, first).wait()
        fetch(m, 1, second).wait()
        total[m] = wide[0:1] * first[m].astype(jnp.float32) + wide[1:2] * second[m].astype(jnp.float32)
        store(m).start()

    @pl.loop(0, M)
    def _(m):
        store(m).wait()


def shards(right_side, coupling, harmonic_offsets, eigen_basis, eigen_inverse, eigen_size):
    vmem = pl.BlockSpec(memory_space=pltpu.VMEM)
    anywhere = pl.BlockSpec(memory_space=pl.ANY)
    low, full = jnp.bfloat16, jnp.float32
    dma = pltpu.SemaphoreType.DMA
    back, steps = pl.pallas_call(
        kernel,
        out_shape=(jax.ShapeDtypeStruct((2, M, ROWS, KZ * R), low), jax.ShapeDtypeStruct((2, 128), full)),
        in_specs=[pl.BlockSpec(memory_space=pltpu.SMEM), anywhere, anywhere, vmem, vmem, vmem],
        out_specs=(anywhere, vmem),
        scratch_shapes=[
            pltpu.VMEM((M, NC, COLS), full),
            pltpu.VMEM((M, NC, COLS), full),
            pltpu.VMEM((M, NC, COLS), full),
            pltpu.VMEM((M, NC, COLS), full),
            pltpu.VMEM((M, H, NC, NC), low),
            pltpu.VMEM((2, M + 2 * OFF, NC, COLS), low),
            pltpu.VMEM((2, 8, COLS), full),
            pltpu.VMEM((2, 1, 128), full),
            pltpu.VMEM((2, 2 * NZ, 1, 128), full),
            pltpu.VMEM((2, 1, 128), full),
            pltpu.VMEM((2, NX // 2, 1, 128), full),
            dma((1,)),
            dma((M,)),
            dma((M,)),
            dma((M,)),
            dma((2,)),
            dma((2,)),
            dma((2,)),
            dma((2, 2 * OFF)),
            dma((2, 2 * OFF)),
            dma((M, 2)),
            dma((M, 4)),
            dma((M, 4)),
            dma((M, 2)),
            dma((2,)),
            dma((2,)),
            dma((2,)),
            dma((2,)),
        ],
        compiler_params=pltpu.CompilerParams(
            collective_id=0, has_side_effects=True, vmem_limit_bytes=56 * 2**20
        ),
    )(harmonic_offsets, right_side, coupling, eigen_basis, eigen_inverse, eigen_size.reshape(1, NC))
    return pl.pallas_call(
        combine,
        out_shape=jax.ShapeDtypeStruct((M, ROWS, KZ * R), full),
        in_specs=[vmem, anywhere],
        out_specs=anywhere,
        scratch_shapes=[
            pltpu.VMEM((M, ROWS, KZ * R), low),
            pltpu.VMEM((M, ROWS, KZ * R), low),
            pltpu.VMEM((M, ROWS, KZ * R), full),
            dma((2, M)),
            dma((M,)),
        ],
    )(steps, back)


def solution(mesh):
    in_specs = (P("sx", "sz", None), P("sx", None, None, None), P(), P(), P(), P())
    out_specs = P("sx", "sz", None)
    return jax.shard_map(shards, mesh=mesh, in_specs=in_specs, out_specs=out_specs, check_vma=False)
```
